1024 devices in a mesh: sec: 2 (over core), tile: 512 (over x, z, y).
Axes of the slice: x: 8, y: 8, z: 8, core: 2. Of those that a mesh axis runs over, the one named last changes fastest.
Arguments:
- velocity: float32 [3, 2048, 128, 128], P(None, 'tile', 'sec'), may hold values from -6 to 6
- stresses: float32 [6, 2048, 128, 128], P(None, 'tile', 'sec'), may hold values from -6 to 6
- buoyancy: float32 [2048, 128, 128], P('tile', 'sec'), may hold values from 0.5 to 1.5
- lame_first: float32 [2048, 128, 128], P('tile', 'sec'), may hold values from 0.5 to 1.5
- shear_mod: float32 [2048, 128, 128], P('tile', 'sec'), may hold values from 0.3 to 1
- ocean_state: float32 [3, 32768, 512], P(None, 'tile', 'sec'), may hold values from -6 to 6
- depth_map: float32 [32768, 512], P('tile', 'sec'), may hold values from 0.5 to 2
- wet_mask: int32 [32768, 512], P('tile', 'sec'), may hold values 0 or 1
- intersection_src: int32 [32768], P('tile'), may hold values from 0 to 511, as said below
- intersection_share: float32 [32768], P('tile'), may hold values from 0.3 to 1
Outputs:
- velocity_out: float32 [3, 2048, 128, 128], P(None, 'tile', 'sec')
- stress_out: float32 [6, 2048, 128, 128], P(None, 'tile', 'sec')
- ocean_out: float32 [3, 32768, 512], P(None, 'tile', 'sec')
The draws below stay inside these ranges and needn't reach their ends.
Inputs may be any that keep to these rules, and one draw needn't show every extreme that they name: intersection_src[r] differs from r // 64 by at most 2.
All inputs are finite; a program needn't handle non-finite values. No bound on the sum of `wet_mask` on one device may be relied on, other than what follows from the above.
Results may differ from the reference program's by a relative error of at most 0.000096.
Values sent between devices are 32-bit elements; how exact they have to be, the bound alone decides.
A program may use at most 32 MiB of HBM per device.

```python
import math
import jax
import jax.numpy as jnp

CX = 4
CY = 64
NZ = 128
OCX = 64
STEPS = 2
OSTEPS = 2
REACH = 2
NX = 2048
NY = 128
OX = 32768
OY = 512
N_SEC = 2
N_TILE = 512


def draw_intersection_src(key, part):
    tiles = jnp.arange(OX, dtype=jnp.int32) // OCX
    offsets = jax.random.randint(key, (OX,), -REACH, REACH + 1, dtype=jnp.int32)
    return jnp.clip(tiles + offsets, 0, OX // OCX - 1).astype(jnp.int32)


def touch_ends(entries, key, smallest, largest):
    place = [jax.random.randint(jax.random.fold_in(key, axis), (), 0, length) for axis, length in enumerate(entries.shape)]
    widest = entries.shape.index(max(entries.shape))
    beside = place[:widest] + [(place[widest] + 1) % entries.shape[widest]] + place[widest + 1:]
    return entries.at[tuple(place)].set(smallest).at[tuple(beside)].set(largest)


def level_of(stream_key, dims, cuts, low, top_value):
    def one(dim, blocks):
        steps = jax.random.uniform(jax.random.fold_in(jax.random.fold_in(stream_key, 6), dim), (blocks,), jnp.float32, low / len(cuts), top_value / len(cuts))
        return jnp.repeat(jnp.exp(steps), dims[dim] // blocks).reshape((-1,) + (1,) * (len(dims) - dim - 1))

    gain = one(*cuts[0])
    for cut in cuts[1:]:
        gain = gain * one(*cut)
    return gain


def noise(own_key, shape, width, bound, pieces=(), kind=jnp.bfloat16):
    loudness = level_of(own_key, shape, pieces, -0.22, 0.18) if pieces else 1.0
    values = jax.random.normal(own_key, shape, jnp.float32) * width * loudness
    return jnp.minimum(jnp.maximum(values, -bound), bound).astype(kind)


def setup_inputs(seed: int = 0) -> dict:
    key_list = jax.random.split(jax.random.key(seed), 11)
    return {
        "velocity": noise(key_list[0], (3, NX, NY, NZ), 1.0, 6.0, ((1, 512), (2, 2)), jnp.float32),
        "stresses": noise(key_list[1], (6, NX, NY, NZ), 1.0, 6.0, ((1, 512), (2, 2)), jnp.float32),
        "buoyancy": jnp.clip(0.5 + 1.0 * jax.random.uniform(key_list[2], (NX, NY, NZ), jnp.float32) ** level_of(key_list[2], (NX, NY, NZ), ((0, 512), (1, 2)), -0.2, 0.2), 0.5, 1.5),
        "lame_first": jnp.clip(0.5 + 1.0 * jax.random.uniform(key_list[3], (NX, NY, NZ), jnp.float32) ** level_of(key_list[3], (NX, NY, NZ), ((0, 512), (1, 2)), -0.2, 0.2), 0.5, 1.5),
        "shear_mod": jnp.clip(0.3 + 0.7 * jax.random.uniform(key_list[4], (NX, NY, NZ), jnp.float32) ** level_of(key_list[4], (NX, NY, NZ), ((0, 512), (1, 2)), -0.2, 0.2), 0.3, 1.0),
        "ocean_state": noise(key_list[5], (3, OX, OY), 1.0, 6.0, ((1, 512), (2, 2)), jnp.float32),
        "depth_map": jnp.clip(jnp.exp(math.log(2.0) - 1.3862944 * jax.random.uniform(key_list[6], (OX, OY), jnp.float32) ** level_of(key_list[6], (OX, OY), ((0, 512), (1, 2)), -0.2, 0.2)), 0.5, 2.0),
        "wet_mask": touch_ends((jax.random.randint(key_list[7], (OX, OY), 0, 8) < 7).astype(jnp.int32), jax.random.fold_in(key_list[7], 1), 0, 1),
        "intersection_src": draw_intersection_src(jax.random.fold_in(key_list[10], 71), 0),
        "intersection_share": jnp.clip(0.3 + 0.7 * jax.random.uniform(key_list[9], (OX,), jnp.float32) ** level_of(key_list[9], (OX,), ((0, 512),), -0.2, 0.2), 0.3, 1.0),
    }


NEAR_COEF = 9.0 / 8.0
FAR_COEF = -1.0 / 24.0
TIME_STEP = 0.15
OCEAN_STEP = 0.3


def offset_slice(field, shift, dimension):
    window = []
    for current in range(3):
        displaced = shift if current == dimension else 0
        window.append(slice(2 + displaced, field.shape[current] - 2 + displaced))
    return field[tuple(window)]


def forward_diff(field, dimension):
    return NEAR_COEF * (offset_slice(field, 1, dimension) - offset_slice(field, 0, dimension)) + FAR_COEF * (offset_slice(field, 2, dimension) - offset_slice(field, -1, dimension))


def backward_diff(field, dimension):
    return NEAR_COEF * (offset_slice(field, 0, dimension) - offset_slice(field, -1, dimension)) + FAR_COEF * (offset_slice(field, 1, dimension) - offset_slice(field, -2, dimension))


def update_velocity(velocity, stress_pad, buoyancy):
    accel_x = forward_diff(stress_pad[0], 0) + backward_diff(stress_pad[3], 1) + backward_diff(stress_pad[4], 2)
    accel_y = backward_diff(stress_pad[3], 0) + forward_diff(stress_pad[1], 1) + backward_diff(stress_pad[5], 2)
    accel_z = backward_diff(stress_pad[4], 0) + backward_diff(stress_pad[5], 1) + forward_diff(stress_pad[2], 2)
    return velocity + TIME_STEP * buoyancy * jnp.stack([accel_x, accel_y, accel_z])


def update_stress(stresses, velocity_pad, lame_first, shear_mod):
    strain_x = backward_diff(velocity_pad[0], 0)
    strain_y = backward_diff(velocity_pad[1], 1)
    strain_z = backward_diff(velocity_pad[2], 2)
    volume = strain_x + strain_y + strain_z
    normal_x = stresses[0] + TIME_STEP * (lame_first * volume + 2.0 * shear_mod * strain_x)
    normal_y = stresses[1] + TIME_STEP * (lame_first * volume + 2.0 * shear_mod * strain_y)
    normal_z = stresses[2] + TIME_STEP * (lame_first * volume + 2.0 * shear_mod * strain_z)
    shear_xy = stresses[3] + TIME_STEP * shear_mod * (forward_diff(velocity_pad[0], 1) + forward_diff(velocity_pad[1], 0))
    shear_xz = stresses[4] + TIME_STEP * shear_mod * (forward_diff(velocity_pad[0], 2) + forward_diff(velocity_pad[2], 0))
    shear_yz = stresses[5] + TIME_STEP * shear_mod * (forward_diff(velocity_pad[1], 2) + forward_diff(velocity_pad[2], 1))
    return jnp.stack([normal_x, normal_y, normal_z, shear_xy, shear_xz, shear_yz])


def pad_all(stacked):
    return jnp.pad(stacked, ((0, 0), (2, 2), (2, 2), (2, 2)))


def ocean_step(ocean_state, depth_map, wet_float, source):
    surface = ocean_state[0]
    padded = jnp.pad(surface, 1)
    grad_x = (padded[2:, 1:-1] - padded[:-2, 1:-1]) * 0.5
    grad_y = (padded[1:-1, 2:] - padded[1:-1, :-2]) * 0.5
    flow_x = wet_float * (ocean_state[1] - OCEAN_STEP * grad_x)
    flow_y = wet_float * (ocean_state[2] - OCEAN_STEP * grad_y)
    flux_pad = jnp.pad(jnp.stack([depth_map * flow_x, depth_map * flow_y]), ((0, 0), (1, 1), (1, 1)))
    spread = (flux_pad[0, 2:, 1:-1] - flux_pad[0, :-2, 1:-1]) * 0.5 + (flux_pad[1, 1:-1, 2:] - flux_pad[1, 1:-1, :-2]) * 0.5
    surface = surface - OCEAN_STEP * spread + OCEAN_STEP * source
    return jnp.stack([surface, flow_x, flow_y])


def reference(velocity, stresses, buoyancy, lame_first, shear_mod, ocean_state, depth_map, wet_mask, intersection_src, intersection_share):
    velocity_out = velocity
    stress_out = stresses
    for step_index in range(STEPS):
        velocity_out = update_velocity(velocity_out, pad_all(stress_out), buoyancy)
        stress_out = update_stress(stress_out, pad_all(velocity_out), lame_first, shear_mod)
    seafloor = velocity_out[2, :, :, 0].reshape(N_TILE, CX, N_SEC, CY).transpose(0, 2, 1, 3).reshape(N_TILE, N_SEC, CX * CY)
    uplift = seafloor[intersection_src.astype(jnp.int32)].reshape(OX, OY)
    wet_float = wet_mask.astype(jnp.float32)
    source = intersection_share[:, None] * wet_float * uplift
    ocean_out = ocean_state
    for step_index in range(OSTEPS):
        ocean_out = ocean_step(ocean_out, depth_map, wet_float, source)
    return (velocity_out, stress_out, ocean_out)
```

```python
import functools

import jax
import jax.numpy as jnp
from jax import lax
from jax.experimental import pallas as pl
from jax.experimental.pallas import tpu as pltpu
from jax.sharding import PartitionSpec as P

REACH = 2
FAR_REACH = REACH + 1
NEAR_COEF = 9.0 / 8.0
FAR_COEF = -1.0 / 24.0
TIME_STEP = 0.15
OCEAN_STEP = 0.3
MESH = pl.DeviceIdType.MESH

YY, YZ, XY, XZ, XX, ZZ = range(6)
SOURCE = (1, 5, 3, 4, 0, 2)

PAD = 8
LAY = 2


def lane_coefs(shape):
    lane = lax.broadcasted_iota(jnp.int32, shape, len(shape) - 1)
    last = shape[-1] - 1

    def coef(value, keep):
        return jnp.where(keep, jnp.float32(value), jnp.float32(0.0))

    forward = (
        coef(NEAR_COEF, lane < last),
        coef(FAR_COEF, lane < last - 1),
        coef(-FAR_COEF, lane > 0),
    )
    backward = (
        coef(-NEAR_COEF, lane > 0),
        coef(FAR_COEF, lane < last),
        coef(-FAR_COEF, lane > 1),
    )
    return forward, backward


def forward_z(f, coefs):
    n, axis = f.shape[-1], f.ndim - 1
    one, two, back = coefs
    return (
        one * pltpu.roll(f, n - 1, axis)
        - NEAR_COEF * f
        + two * pltpu.roll(f, n - 2, axis)
        + back * pltpu.roll(f, 1, axis)
    )


def backward_z(f, coefs):
    n, axis = f.shape[-1], f.ndim - 1
    back, one, two = coefs
    return (
        NEAR_COEF * f
        + back * pltpu.roll(f, 1, axis)
        + one * pltpu.roll(f, n - 1, axis)
        + two * pltpu.roll(f, 2, axis)
    )


def kernel(
    tiles,
    vel_in, str_in, buo_in, lam_in, mu_in, oce_in, dep_in, wet_in, src_in, share_in,
    vel_out, str_out, oce_out,
    s0, s1, v0, v1, v2, buo, lam, mu,
    src, share, oce, dep, wet, loc, locn, pat, row, flux, vel1,
    load_sem, xs_sem, xr_sem, ys_sem, yr_sem, os_sem, or_sem, ps_sem, pr_sem,
):
    cx, cy, nz = buo_in.shape
    ocx, ocy = dep_in.shape
    half = ocy // 2
    tile = lax.axis_index("tile")
    sec = lax.axis_index("sec")
    has_low = tile > 0
    has_high = tile < tiles - 1
    own = pl.ds(LAY, cx)
    rows_own = pl.ds(PAD, cy)
    orow_own = pl.ds(PAD, ocx)

    def device(step, other=False):
        return {"sec": 1 - sec if other else sec, "tile": tile + step}

    loads = [
        pltpu.make_async_copy(str_in.at[SOURCE[c]], s0.at[c, own, rows_own], load_sem.at[c])
        for c in range(6)
    ]
    loads += [
        pltpu.make_async_copy(vel_in, v0, load_sem.at[6]),
        pltpu.make_async_copy(buo_in, buo, load_sem.at[7]),
        pltpu.make_async_copy(lam_in, lam, load_sem.at[8]),
        pltpu.make_async_copy(mu_in, mu, load_sem.at[9]),
    ]
    ocean_loads = [
        pltpu.make_async_copy(oce_in, oce.at[:, orow_own, 0:ocy], load_sem.at[10]),
        pltpu.make_async_copy(dep_in, dep.at[orow_own, 0:ocy], load_sem.at[11]),
        pltpu.make_async_copy(wet_in, wet.at[orow_own, 0:ocy], load_sem.at[12]),
    ]
    row_loads = [
        pltpu.make_async_copy(src_in, src, load_sem.at[13]),
        pltpu.make_async_copy(share_in, share, load_sem.at[14]),
    ]
    for copy in row_loads + loads + ocean_loads:
        copy.start()

    outer = pl.multiple_of((cy + PAD) * sec, 8)
    for field in (s0, s1):
        field[0:3, own, pl.ds(outer, PAD), :] = jnp.zeros((3, cx, PAD, nz), jnp.float32)
    for field in (v1, v2):
        field[:, own, pl.ds(outer, PAD), :] = jnp.zeros((3, cx, PAD, nz), jnp.float32)
    pat[...] = jnp.zeros(pat.shape, jnp.float32)

    def clear(layers, orow, slot):
        for field in (s0, s1):
            field[XY : XX + 1, layers, rows_own, :] = jnp.zeros((3, LAY, cy, nz), jnp.float32)
        for field in (v1, v2):
            field[:, layers, rows_own, :] = jnp.zeros((3, LAY, cy, nz), jnp.float32)
        oce[:, orow, 0:ocy] = jnp.zeros((3, PAD, ocy), jnp.float32)
        dep[orow, 0:ocy] = jnp.zeros((PAD, ocy), jnp.float32)
        wet[orow, 0:ocy] = jnp.zeros((PAD, ocy), jnp.int32)
        locn[slot] = jnp.zeros(locn.shape[1:], jnp.float32)

    @pl.when(jnp.logical_not(has_low))
    def _():
        clear(slice(0, LAY), slice(0, PAD), 0)

    @pl.when(jnp.logical_not(has_high))
    def _():
        clear(slice(LAY + cx, LAY + cx + LAY), slice(PAD + ocx, PAD + ocx + PAD), 1)

    barrier = pltpu.get_barrier_semaphore()
    pl.semaphore_signal(barrier, inc=1, device_id=device(0, True), device_id_type=MESH)

    @pl.when(has_low)
    def _():
        pl.semaphore_signal(barrier, inc=1, device_id=device(-1), device_id_type=MESH)

    @pl.when(has_high)
    def _():
        pl.semaphore_signal(barrier, inc=1, device_id=device(1), device_id_type=MESH)

    pl.semaphore_wait(barrier, 1 + has_low.astype(jnp.int32) + has_high.astype(jnp.int32))

    def copy_to(source, target, send, receive, where):
        return pltpu.make_async_remote_copy(
            src_ref=source, dst_ref=target, send_sem=send, recv_sem=receive,
            device_id=where, device_id_type=MESH,
        )

    low, high = LAY, LAY + cx

    def x_copies(number, field, source=None):
        up, down = [], []
        if number % 2 == 0:
            if source is None:
                near = field.at[XX, :, rows_own]
                far = field.at[XY : XZ + 1, :, rows_own]
                shift = 0
            else:
                near = source.at[SOURCE[XX]]
                far = source.at[SOURCE[XY] : SOURCE[XZ] + 1]
                shift = LAY
            ups = [
                (near.at[high - 1 - shift : high - shift], field.at[XX, 1:2, rows_own]),
                (far.at[:, high - 2 - shift : high - shift], field.at[XY : XZ + 1, 0:2, rows_own]),
            ]
            downs = [
                (near.at[low - shift : low + 2 - shift], field.at[XX, high : high + 2, rows_own]),
                (far.at[:, low - shift : low + 1 - shift], field.at[XY : XZ + 1, high : high + 1, rows_own]),
            ]
        else:
            near = field.at[0, :, rows_own]
            far = field.at[1:3, :, rows_own]
            ups = [
                (near.at[high - 2 : high], field.at[0, 0:2, rows_own]),
                (far.at[:, high - 1 : high], field.at[1:3, 1:2, rows_own]),
            ]
            downs = [
                (near.at[low : low + 1], field.at[0, high : high + 1, rows_own]),
                (far.at[:, low : low + 2], field.at[1:3, high : high + 2, rows_own]),
            ]
        for i, (a, b) in enumerate(ups):
            up.append(copy_to(a, b, xs_sem.at[number, 0, i], xr_sem.at[number, 0, i], device(1)))
        for i, (a, b) in enumerate(downs):
            down.append(copy_to(a, b, xs_sem.at[number, 1, i], xr_sem.at[number, 1, i], device(-1)))
        return up, down

    def start(copies):
        up, down = copies

        @pl.when(has_high)
        def _():
            for copy in up:
                copy.start()

        @pl.when(has_low)
        def _():
            for copy in down:
                copy.start()

    def arrive(copies):
        up, down = copies

        @pl.when(has_low)
        def _():
            for copy in up:
                copy.wait_recv()

        @pl.when(has_high)
        def _():
            for copy in down:
                copy.wait_recv()

    def sent(copies):
        up, down = copies

        @pl.when(has_high)
        def _():
            for copy in up:
                copy.wait_send()

        @pl.when(has_low)
        def _():
            for copy in down:
                copy.wait_send()

    y_from = pl.multiple_of(cy - (cy - PAD) * sec, 8)
    y_to = pl.multiple_of((cy + PAD) * sec, 8)

    def y_copy(number, field):
        part = field.at[0:3, own]
        return copy_to(
            part.at[:, :, pl.ds(y_from, PAD)],
            part.at[:, :, pl.ds(y_to, PAD)],
            ys_sem.at[number], yr_sem.at[number], device(0, True),
        )

    x_s0 = x_copies(0, s0, str_in)
    start(x_s0)

    loc[...] = jnp.zeros(loc.shape, jnp.float32)
    for copy in row_loads:
        copy.wait()
    loc[0:1, 0:ocx] = src[...].astype(jnp.float32)
    loc[1:2, 0:ocx] = share[...]

    def ocean_rows(step, first, target, slot, index):
        return [
            copy_to(oce_in.at[:, pl.ds(first, PAD)], oce.at[:, pl.ds(target, PAD), 0:ocy], os_sem.at[index, 0], or_sem.at[index, 0], device(step)),
            copy_to(dep_in.at[pl.ds(first, PAD)], dep.at[pl.ds(target, PAD), 0:ocy], os_sem.at[index, 1], or_sem.at[index, 1], device(step)),
            copy_to(wet_in.at[pl.ds(first, PAD)], wet.at[pl.ds(target, PAD), 0:ocy], os_sem.at[index, 2], or_sem.at[index, 2], device(step)),
            copy_to(loc, locn.at[slot], os_sem.at[index, 3], or_sem.at[index, 3], device(step)),
        ]

    x_ocean = (
        ocean_rows(1, ocx - PAD, 0, 0, 0),
        ocean_rows(-1, 0, PAD + ocx, 1, 1),
    )
    start(x_ocean)

    for copy in loads:
        copy.wait()
    y_s0 = y_copy(0, s0)
    y_s0.start()

    forward, backward = lane_coefs((1, 1, nz))

    def forward_x(a):
        return NEAR_COEF * (a[2 : 2 + cx] - a[1 : 1 + cx]) + FAR_COEF * (a[3 : 3 + cx] - a[0:cx])

    def backward_x(a):
        return NEAR_COEF * (a[2 : 2 + cx] - a[1 : 1 + cx]) + FAR_COEF * (a[3 : 3 + cx] - a[0:cx])

    def velocity_rows(i, old, stress, new, out=None):
        base = pl.multiple_of(PAD + i * 8, 8)
        here = pl.ds(pl.multiple_of(i * 8, 8), 8)

        def at(c, layers, shift=0):
            return stress[c, layers, pl.ds(base + shift, 8), :]

        def fy(c):
            return NEAR_COEF * (at(c, own, 1) - at(c, own)) + FAR_COEF * (at(c, own, 2) - at(c, own, -1))

        def by(c):
            return NEAR_COEF * (at(c, own) - at(c, own, -1)) + FAR_COEF * (at(c, own, 1) - at(c, own, -2))

        def fx(c):
            return forward_x(at(c, pl.ds(LAY - 1, cx + 3)))

        def bx(c):
            return backward_x(at(c, pl.ds(LAY - 2, cx + 3)))

        scale = TIME_STEP * buo[:, here, :]
        x = fx(XX) + by(XY) + backward_z(at(XZ, own), backward)
        y = bx(XY) + fy(YY) + backward_z(at(YZ, own), backward)
        z = bx(XZ) + by(YZ) + forward_z(at(ZZ, own), forward)
        if old is v0:
            before = old[:, :, here, :]
        else:
            before = old[:, own, pl.ds(base, 8), :]
        for c, value in enumerate((x, y, z)):
            result = before[c] + scale * value
            new[c, own, pl.ds(base, 8), :] = result
            if out is not None:
                out[c, :, here, :] = result

    def stress_rows(i, old, velocity, new, last):
        base = pl.multiple_of(PAD + i * 8, 8)
        here = pl.ds(pl.multiple_of(i * 8, 8), 8)

        def at(c, layers, shift=0):
            return velocity[c, layers, pl.ds(base + shift, 8), :]

        def fy(c):
            return NEAR_COEF * (at(c, own, 1) - at(c, own)) + FAR_COEF * (at(c, own, 2) - at(c, own, -1))

        def by(c):
            return NEAR_COEF * (at(c, own) - at(c, own, -1)) + FAR_COEF * (at(c, own, 1) - at(c, own, -2))

        def fx(c):
            return forward_x(at(c, pl.ds(LAY - 1, cx + 3)))

        strain_x = backward_x(at(0, pl.ds(LAY - 2, cx + 3)))
        strain_y = by(1)
        strain_z = backward_z(at(2, own), backward)
        shear = TIME_STEP * mu[:, here, :]
        volume = TIME_STEP * lam[:, here, :] * (strain_x + strain_y + strain_z)
        change = {
            XX: volume + 2.0 * shear * strain_x,
            YY: volume + 2.0 * shear * strain_y,
            ZZ: volume + 2.0 * shear * strain_z,
            XY: shear * (fy(0) + fx(1)),
            XZ: shear * (forward_z(at(0, own), forward) + fx(2)),
            YZ: shear * (forward_z(at(1, own), forward) + fy(2)),
        }
        for c, value in change.items():
            result = old[c, own, pl.ds(base, 8), :] + value
            if last:
                new[SOURCE[c], :, here, :] = result
            else:
                new[c, own, pl.ds(base, 8), :] = result

    def each(function, *args):
        def body(i, carry):
            function(i, *args)
            return carry

        lax.fori_loop(0, cy // 8, body, 0)

    y_s0.wait_recv()
    arrive(x_s0)
    each(velocity_rows, v0, s0, v1)
    x_v1, y_v1 = x_copies(1, v1), y_copy(1, v1)
    start(x_v1)
    y_v1.start()

    for copy in ocean_loads:
        copy.wait()
    arrive(x_ocean)
    edge = pl.multiple_of(half * (1 - sec), 128)

    def ocean_columns(field, index):
        part = field.at[:, :, :] if len(field.shape) == 3 else field.at[:, :]
        if len(field.shape) == 3:
            a, b = part.at[:, :, pl.ds(edge, half)], part.at[:, :, ocy : ocy + half]
        else:
            a, b = part.at[:, pl.ds(edge, half)], part.at[:, ocy : ocy + half]
        return copy_to(a, b, os_sem.at[2, index], or_sem.at[2, index], device(0, True))

    y_ocean = [ocean_columns(oce, 0), ocean_columns(dep, 1), ocean_columns(wet, 2)]
    for copy in y_ocean:
        copy.start()

    lane = lax.broadcasted_iota(jnp.int32, (8, 128), 1)

    def spread(value):
        return jnp.broadcast_to(value, (8, 128))

    def lanes_of(index):
        mine = pltpu.roll(spread(loc[index : index + 1, :]), PAD, 1)
        below = pltpu.roll(spread(locn[0, index : index + 1, :]), 128 - (ocx - PAD), 1)
        above = pltpu.roll(spread(locn[1, index : index + 1, :]), PAD + ocx, 1)
        return jnp.where(lane < PAD, below, jnp.where(lane < PAD + ocx, mine, above))

    slot = lax.broadcasted_iota(jnp.int32, (8, 128), 0)
    picked = lanes_of(0).astype(jnp.int32) - tile + FAR_REACH == slot
    row[...] = jnp.where(picked, OCEAN_STEP * lanes_of(1), 0.0)

    y_v1.wait_recv()
    arrive(x_v1)
    each(stress_rows, s0, v1, s1, False)
    x_s1, y_s1 = x_copies(2, s1), y_copy(2, s1)
    start(x_s1)
    y_s1.start()

    for copy in y_ocean:
        copy.wait()
    region = oce.shape[1:]
    width = region[1]
    lanes = lax.broadcasted_iota(jnp.int32, (1, width), 1)
    beyond = lanes - ocy
    inside = (beyond < 0) | ((beyond < half // 2) & (sec == 0)) | ((beyond >= half // 2) & (sec == 1))
    rows = lax.broadcasted_iota(jnp.int32, (region[0], 1), 0)
    inside_rows = ((rows >= PAD) | has_low) & ((rows < PAD + ocx) | has_high)
    mask = inside.astype(jnp.float32) * inside_rows.astype(jnp.float32)
    wetf = wet[...].astype(jnp.float32) * mask
    vel1[3] = wetf
    oce[0] = oce[0] * mask
    HALF_STEP = 0.5 * OCEAN_STEP

    def ocean_flow(eta, u, v, first, count, out_u, out_v):
        here = pl.ds(first, count)
        middle = eta[here, :]
        w = vel1[3, here, :]
        new_u = w * (u[here, :] - HALF_STEP * (eta[pl.ds(first + 1, count), :] - eta[pl.ds(first - 1, count), :]))
        new_v = w * (v[here, :] - HALF_STEP * (pltpu.roll(middle, width - 1, 1) - pltpu.roll(middle, 1, 1)))
        out_u[here, :] = new_u
        out_v[here, :] = new_v
        flux[0, here, :] = dep[here, :] * new_u
        flux[1, here, :] = dep[here, :] * new_v

    def ocean_fall(first, count):
        along = flux[1, pl.ds(first, count), :]
        return HALF_STEP * (
            flux[0, pl.ds(first + 1, count), :] - flux[0, pl.ds(first - 1, count), :]
            + pltpu.roll(along, width - 1, 1) - pltpu.roll(along, 1, 1)
        )

    ocean_flow(oce.at[0], oce.at[1], oce.at[2], 4, ocx + 8, vel1.at[0], vel1.at[1])
    here = pl.ds(5, ocx + 6)
    rows_here = lax.broadcasted_iota(jnp.int32, (ocx + 6, 1), 0) + 5
    mask_here = inside.astype(jnp.float32) * (
        ((rows_here >= PAD) | has_low) & ((rows_here < PAD + ocx) | has_high)
    ).astype(jnp.float32)
    vel1[2, here, :] = (oce[0, here, :] - ocean_fall(5, ocx + 6)) * mask_here

    y_s1.wait_recv()
    arrive(x_s1)
    each(velocity_rows, v1, s1, v2, vel_out)
    x_v2, y_v2 = x_copies(3, v2), y_copy(3, v2)
    start(x_v2)
    y_v2.start()

    top = v2[2, own, rows_own, :].reshape(cx * cy, nz)
    first_lane = (lax.broadcasted_iota(jnp.int32, (8, nz), 1) == 0).astype(jnp.float32)
    patch = lax.dot_general(
        first_lane, top, (((1,), (1,)), ((), ())),
        precision=lax.Precision.HIGHEST, preferred_element_type=jnp.float32,
    )
    pat[8:16, 0:ocy] = patch
    patch_copies = []
    for other in (False, True):
        for step in range(-FAR_REACH, FAR_REACH + 1):
            if step == 0 and not other:
                continue
            index = FAR_REACH - step
            if other:
                source = pat.at[8:9, pl.ds(edge, half)]
                target = pat.at[index : index + 1, ocy : ocy + half]
            else:
                source = pat.at[8:9, 0:ocy]
                target = pat.at[index : index + 1, 0:ocy]
            copy = copy_to(source, target, ps_sem.at[int(other), index], pr_sem.at[int(other), index], device(step, other))
            back = (tile - step >= 0) & (tile - step < tiles)
            ahead = (tile + step >= 0) & (tile + step < tiles)
            patch_copies.append((copy, ahead, back))
    for copy, ahead, back in patch_copies:
        pl.when(ahead)(copy.start)
    pat[FAR_REACH : FAR_REACH + 1, 0:ocy] = patch[0:1]

    y_v2.wait_recv()
    arrive(x_v2)
    each(stress_rows, s1, v2, str_out, True)

    for copy, ahead, back in patch_copies:
        pl.when(back)(copy.wait_recv)
    uplift = lax.dot_general(
        row[...], pat[0:8, :], (((0,), (0,)), ((), ())),
        precision=lax.Precision.HIGHEST, preferred_element_type=jnp.float32,
    )[0 : PAD + ocx + PAD]
    source = vel1[3] * uplift
    oce[0] = vel1[2] + source
    ocean_flow(oce.at[0], vel1.at[0], vel1.at[1], PAD - 1, ocx + 2, oce.at[1], oce.at[2])
    oce_out[0] = oce[0, orow_own, 0:ocy] - ocean_fall(PAD, ocx)[:, 0:ocy] + source[PAD : PAD + ocx, 0:ocy]
    oce_out[1:3] = oce[1:3, orow_own, 0:ocy]

    for copies in (x_s0, x_ocean, x_v1, x_s1, x_v2):
        sent(copies)
    for copy in (y_s0, y_v1, y_s1, y_v2):
        copy.wait_send()
    for copy, ahead, back in patch_copies:
        pl.when(ahead)(copy.wait_send)


def solution(mesh):
    tiles = mesh.shape["tile"]

    def shards(velocity, stresses, buoyancy, lame_first, shear_mod, ocean_state, depth_map, wet_mask, src, share):
        cx, cy, nz = buoyancy.shape
        ocx, ocy = depth_map.shape
        layers, rows = cx + 2 * LAY, cy + 2 * PAD
        region = (ocx + 2 * PAD, ocy + ocy // 2)
        hbm = pl.BlockSpec(memory_space=pltpu.HBM)
        vmem = pl.BlockSpec(memory_space=pltpu.VMEM)
        dma = pltpu.SemaphoreType.DMA
        f32 = jnp.float32
        return pl.pallas_call(
            functools.partial(kernel, tiles),
            out_shape=(
                jax.ShapeDtypeStruct(velocity.shape, f32),
                jax.ShapeDtypeStruct(stresses.shape, f32),
                jax.ShapeDtypeStruct(ocean_state.shape, f32),
            ),
            in_specs=[hbm] * 10,
            out_specs=(vmem,) * 3,
            scratch_shapes=[
                pltpu.VMEM((6, layers, rows, nz), f32),
                pltpu.VMEM((6, layers, rows, nz), f32),
                pltpu.VMEM(velocity.shape, f32),
                pltpu.VMEM((3, layers, rows, nz), f32),
                pltpu.VMEM((3, layers, rows, nz), f32),
                pltpu.VMEM(buoyancy.shape, f32),
                pltpu.VMEM(buoyancy.shape, f32),
                pltpu.VMEM(buoyancy.shape, f32),
                pltpu.VMEM((1, ocx), jnp.int32),
                pltpu.VMEM((1, ocx), f32),
                pltpu.VMEM((3, *region), f32),
                pltpu.VMEM(region, f32),
                pltpu.VMEM(region, jnp.int32),
                pltpu.VMEM((8, 128), f32),
                pltpu.VMEM((2, 8, 128), f32),
                pltpu.VMEM((16, region[1]), f32),
                pltpu.VMEM((8, 128), f32),
                pltpu.VMEM((2, *region), f32),
                pltpu.VMEM((4, *region), f32),
                dma((15,)),
                dma((4, 2, 2)),
                dma((4, 2, 2)),
                dma((4,)),
                dma((4,)),
                dma((3, 4)),
                dma((3, 4)),
                dma((2, 7)),
                dma((2, 7)),
            ],
            compiler_params=pltpu.CompilerParams(
                collective_id=0, has_side_effects=True, vmem_limit_bytes=40 * 1024 * 1024
            ),
        )(
            *(
                pltpu.with_memory_space_constraint(array, pltpu.HBM)
                for array in (
                    velocity, stresses, buoyancy, lame_first, shear_mod, ocean_state, depth_map, wet_mask,
                    src.reshape(1, ocx), share.reshape(1, ocx),
                )
            )
        )

    return jax.shard_map(
        shards,
        mesh=mesh,
        in_specs=(
            P(None, "tile", "sec", None),
            P(None, "tile", "sec", None),
            P("tile", "sec", None),
            P("tile", "sec", None),
            P("tile", "sec", None),
            P(None, "tile", "sec"),
            P("tile", "sec"),
            P("tile", "sec"),
            P("tile"),
            P("tile"),
        ),
        out_specs=(
            P(None, "tile", "sec", None),
            P(None, "tile", "sec", None),
            P(None, "tile", "sec"),
        ),
        check_vma=False,
    )
```

```python
import functools

import jax
import jax.numpy as jnp
from jax import lax
from jax.experimental import pallas as pl
from jax.experimental.pallas import tpu as pltpu
from jax.sharding import PartitionSpec as P

REACH = 2
FAR_REACH = REACH + 1
NEAR_COEF = 9.0 / 8.0
FAR_COEF = -1.0 / 24.0
TIME_STEP = 0.15
OCEAN_STEP = 0.3
MESH = pl.DeviceIdType.MESH

YY, YZ, XY, XZ, XX, ZZ = range(6)
SOURCE = (1, 5, 3, 4, 0, 2)

PAD = 8
LAY = 2
BOUNDS = (0, 4, 8)


def lane_coefs(shape):
    lane = lax.broadcasted_iota(jnp.int32, shape, len(shape) - 1)
    last = shape[-1] - 1

    def coef(value, keep):
        return jnp.where(keep, jnp.float32(value), jnp.float32(0.0))

    forward = (
        coef(NEAR_COEF, lane < last),
        coef(FAR_COEF, lane < last - 1),
        coef(-FAR_COEF, lane > 0),
    )
    backward = (
        coef(-NEAR_COEF, lane > 0),
        coef(FAR_COEF, lane < last),
        coef(-FAR_COEF, lane > 1),
    )
    return forward, backward


def forward_z(f, coefs):
    n, axis = f.shape[-1], f.ndim - 1
    one, two, back = coefs
    return (
        one * pltpu.roll(f, n - 1, axis)
        - NEAR_COEF * f
        + two * pltpu.roll(f, n - 2, axis)
        + back * pltpu.roll(f, 1, axis)
    )


def backward_z(f, coefs):
    n, axis = f.shape[-1], f.ndim - 1
    back, one, two = coefs
    return (
        NEAR_COEF * f
        + back * pltpu.roll(f, 1, axis)
        + one * pltpu.roll(f, n - 1, axis)
        + two * pltpu.roll(f, 2, axis)
    )


def kernel(
    tiles,
    vel_in, str_in, buo_in, lam_in, mu_in, oce_in, dep_in, wet_in, src_in, share_in,
    vel_out, str_out, oce_out,
    s0, sp, s1, v0, v1, v2, buo, lam, mu, stiff,
    src, share, oce, dep, wet, loc, locn, pat, row, flux, vel1,
    load_sem, xs_sem, xr_sem, ys_sem, yr_sem, os_sem, or_sem, ps_sem, pr_sem,
):
    cx, cy, nz = buo_in.shape
    ocx, ocy = dep_in.shape
    half = ocy // 2
    tile = lax.axis_index("tile")
    sec = lax.axis_index("sec")
    has_low = tile > 0
    has_high = tile < tiles - 1
    own = pl.ds(LAY, cx)
    rows_own = pl.ds(PAD, cy)
    orow_own = pl.ds(PAD, ocx)

    def device(step, other=False):
        return {"sec": 1 - sec if other else sec, "tile": tile + step}

    loads = [
        pltpu.make_async_copy(str_in.at[SOURCE[c]], s0.at[c, own, rows_own], load_sem.at[c])
        for c in range(6)
    ]
    loads += [
        pltpu.make_async_copy(vel_in, v0, load_sem.at[6]),
        pltpu.make_async_copy(buo_in, buo, load_sem.at[7]),
        pltpu.make_async_copy(lam_in, lam, load_sem.at[8]),
        pltpu.make_async_copy(mu_in, mu.at[own], load_sem.at[9]),
    ]
    ocean_loads = [
        pltpu.make_async_copy(oce_in, oce.at[:, orow_own, 0:ocy], load_sem.at[10]),
        pltpu.make_async_copy(dep_in, dep.at[orow_own, 0:ocy], load_sem.at[11]),
        pltpu.make_async_copy(wet_in, wet.at[orow_own, 0:ocy], load_sem.at[12]),
    ]
    row_loads = [
        pltpu.make_async_copy(src_in, src, load_sem.at[13]),
        pltpu.make_async_copy(share_in, share, load_sem.at[14]),
    ]
    for copy in row_loads + loads + ocean_loads:
        copy.start()

    outer = pl.multiple_of((cy + PAD) * sec, 8)
    for field in (s0, s1):
        field[0:3, own, pl.ds(outer, PAD), :] = jnp.zeros((3, cx, PAD, nz), jnp.float32)
    for field in (v1, v2):
        field[:, own, pl.ds(outer, PAD), :] = jnp.zeros((3, cx, PAD, nz), jnp.float32)
    pat[...] = jnp.zeros(pat.shape, jnp.float32)

    def clear(layers, orow, slot):
        for field in (s0, sp):
            field[XY : XX + 1, layers, rows_own, :] = jnp.zeros((3, LAY, cy, nz), jnp.float32)
        for field in (v1, v2):
            field[:, layers, rows_own, :] = jnp.zeros((3, LAY, cy, nz), jnp.float32)
        for field in (mu, stiff):
            field[layers] = jnp.zeros((LAY, cy, nz), jnp.float32)
        oce[:, orow, 0:ocy] = jnp.zeros((3, PAD, ocy), jnp.float32)
        dep[orow, 0:ocy] = jnp.zeros((PAD, ocy), jnp.float32)
        wet[orow, 0:ocy] = jnp.zeros((PAD, ocy), jnp.int32)
        locn[slot] = jnp.zeros(locn.shape[1:], jnp.float32)

    @pl.when(jnp.logical_not(has_low))
    def _():
        clear(slice(0, LAY), slice(0, PAD), 0)

    @pl.when(jnp.logical_not(has_high))
    def _():
        clear(slice(LAY + cx, LAY + cx + LAY), slice(PAD + ocx, PAD + ocx + PAD), 1)

    barrier = pltpu.get_barrier_semaphore()
    pl.semaphore_signal(barrier, inc=1, device_id=device(0, True), device_id_type=MESH)

    @pl.when(has_low)
    def _():
        pl.semaphore_signal(barrier, inc=1, device_id=device(-1), device_id_type=MESH)

    @pl.when(has_high)
    def _():
        pl.semaphore_signal(barrier, inc=1, device_id=device(1), device_id_type=MESH)

    pl.semaphore_wait(barrier, 1 + has_low.astype(jnp.int32) + has_high.astype(jnp.int32))

    def copy_to(source, target, send, receive, where):
        return pltpu.make_async_remote_copy(
            src_ref=source, dst_ref=target, send_sem=send, recv_sem=receive,
            device_id=where, device_id_type=MESH,
        )

    low, high = LAY, LAY + cx
    groups = cy // 8

    def bounds_after(bounds):
        return [0] + [max(b - 1, 0) for b in bounds[1:-1]] + [groups]

    s0_bounds = list(BOUNDS)
    sp_bounds = bounds_after(s0_bounds)
    v2_bounds = bounds_after(sp_bounds)

    def rows_of(first, last):
        return pl.multiple_of(8 * first + sec * (cy - 8 * first - 8 * last), 8), 8 * (last - first)

    S0, V1, SP, V2, STATIC = range(5)

    def x_copies(number, field, chunk=0, first=0, last=groups, source=None):
        if first == last:
            return [], []
        begin, count = rows_of(first, last)
        rows = pl.ds(PAD + begin, count)
        if number in (S0, SP):
            if source is None:
                near, far = field.at[XX, :, rows], field.at[XY : XZ + 1, :, rows]
                shift = 0
            else:
                near = source.at[SOURCE[XX], :, pl.ds(begin, count)]
                far = source.at[SOURCE[XY] : SOURCE[XZ] + 1, :, pl.ds(begin, count)]
                shift = LAY
            ups = [
                (near.at[high - 1 - shift : high - shift], field.at[XX, 1:2, rows]),
                (far.at[:, high - 2 - shift : high - shift], field.at[XY : XZ + 1, 0:2, rows]),
            ]
            downs = [
                (near.at[low - shift : low + 2 - shift], field.at[XX, high : high + 2, rows]),
                (far.at[:, low - shift : low + 1 - shift], field.at[XY : XZ + 1, high : high + 1, rows]),
            ]
        elif number in (V1, V2):
            near, far = field.at[0, :, rows], field.at[1:3, :, rows]
            ups = [
                (near.at[high - 2 : high], field.at[0, 0:2, rows]),
                (far.at[:, high - 1 : high], field.at[1:3, 1:2, rows]),
            ]
            downs = [
                (near.at[low : low + 1], field.at[0, high : high + 1, rows]),
                (far.at[:, low : low + 2], field.at[1:3, high : high + 2, rows]),
            ]
        else:
            ups = [(stiff.at[high - 1 : high], stiff.at[1:2]), (mu.at[high - 2 : high], mu.at[0:2])]
            downs = [(stiff.at[low : low + 2], stiff.at[high : high + 2]), (mu.at[low : low + 1], mu.at[high : high + 1])]
        up = [
            copy_to(a, b, xs_sem.at[number, chunk, 0, i], xr_sem.at[number, chunk, 0, i], device(1))
            for i, (a, b) in enumerate(ups)
        ]
        down = [
            copy_to(a, b, xs_sem.at[number, chunk, 1, i], xr_sem.at[number, chunk, 1, i], device(-1))
            for i, (a, b) in enumerate(downs)
        ]
        return up, down

    def chunks(number, field, bounds, source=None):
        return [
            x_copies(number, field, i, first, last, source)
            for i, (first, last) in enumerate(zip(bounds[:-1], bounds[1:]))
        ]

    def start(copies):
        up, down = copies

        @pl.when(has_high)
        def _():
            for copy in up:
                copy.start()

        @pl.when(has_low)
        def _():
            for copy in down:
                copy.start()

    def arrive(copies):
        up, down = copies

        @pl.when(has_low)
        def _():
            for copy in up:
                copy.wait_recv()

        @pl.when(has_high)
        def _():
            for copy in down:
                copy.wait_recv()

    def sent(copies):
        up, down = copies

        @pl.when(has_high)
        def _():
            for copy in up:
                copy.wait_send()

        @pl.when(has_low)
        def _():
            for copy in down:
                copy.wait_send()

    y_from = pl.multiple_of(cy - (cy - PAD) * sec, 8)
    y_to = pl.multiple_of((cy + PAD) * sec, 8)

    def y_copy(number, field):
        part = field.at[0:3, own]
        return copy_to(
            part.at[:, :, pl.ds(y_from, PAD)],
            part.at[:, :, pl.ds(y_to, PAD)],
            ys_sem.at[number], yr_sem.at[number], device(0, True),
        )

    x_s0 = chunks(S0, s0, s0_bounds, str_in)
    for part in x_s0:
        start(part)

    loc[...] = jnp.zeros(loc.shape, jnp.float32)
    for copy in row_loads:
        copy.wait()
    loc[0:1, 0:ocx] = src[...].astype(jnp.float32)
    loc[1:2, 0:ocx] = share[...]

    def ocean_rows(step, first, target, slot, index):
        return [
            copy_to(oce_in.at[:, pl.ds(first, PAD)], oce.at[:, pl.ds(target, PAD), 0:ocy], os_sem.at[index, 0], or_sem.at[index, 0], device(step)),
            copy_to(dep_in.at[pl.ds(first, PAD)], dep.at[pl.ds(target, PAD), 0:ocy], os_sem.at[index, 1], or_sem.at[index, 1], device(step)),
            copy_to(wet_in.at[pl.ds(first, PAD)], wet.at[pl.ds(target, PAD), 0:ocy], os_sem.at[index, 2], or_sem.at[index, 2], device(step)),
            copy_to(loc, locn.at[slot], os_sem.at[index, 3], or_sem.at[index, 3], device(step)),
        ]

    x_ocean = (
        ocean_rows(1, ocx - PAD, 0, 0, 0),
        ocean_rows(-1, 0, PAD + ocx, 1, 1),
    )
    for copy in loads:
        copy.wait()
    y_s0 = y_copy(0, s0)
    y_s0.start()

    buo[...] = TIME_STEP * buo[...]
    lam[...] = TIME_STEP * lam[...]
    mu[own] = TIME_STEP * mu[own]
    stiff[own] = lam[...] + 2.0 * mu[own]
    x_static = x_copies(STATIC, None)
    start(x_static)
    start(x_ocean)

    forward, backward = lane_coefs((1, 1, nz))

    def near_far(a, b, c, d):
        return NEAR_COEF * (a - b) + FAR_COEF * (c - d)

    def outer_x(a):
        zero = jnp.zeros_like(a[0:1])
        return jnp.concatenate([zero, zero, a, zero, zero])

    def forward_x(a):
        return near_far(a[3 : 3 + cx], a[2 : 2 + cx], a[4 : 4 + cx], a[1 : 1 + cx])

    def backward_x(a):
        return near_far(a[2 : 2 + cx], a[1 : 1 + cx], a[3 : 3 + cx], a[0:cx])

    every = pl.ds(0, cx + 2 * LAY)

    def place(g):
        begin = pl.multiple_of(8 * (g + sec * (groups - 1 - 2 * g)), 8)
        return pl.ds(begin, 8), begin + PAD

    def velocity_group(g, old, stress, new, halos, out=None):
        here, base = place(g)

        def at(c, layers=own, shift=0):
            return stress[c, layers, pl.ds(base + shift, 8), :]

        def fy(c):
            return near_far(at(c, own, 1), at(c), at(c, own, 2), at(c, own, -1))

        def by(c):
            return near_far(at(c), at(c, own, -1), at(c, own, 1), at(c, own, -2))

        def wide(c):
            return at(c, every) if halos else outer_x(at(c))

        scale = buo[:, here, :]
        x = forward_x(wide(XX)) + by(XY) + backward_z(at(XZ), backward)
        y = backward_x(wide(XY)) + fy(YY) + backward_z(at(YZ), backward)
        z = backward_x(wide(XZ)) + by(YZ) + forward_z(at(ZZ), forward)
        for c, value in enumerate((x, y, z)):
            if halos:
                result = old[c, own, pl.ds(base, 8), :] + scale * value
                new[c, own, pl.ds(base, 8), :] = result
                out[c, :, here, :] = result
            else:
                new[c, :, here, :] = old[c, :, here, :] + scale * value

    def stress_group(g, old, velocity, new, last):
        here, base = place(g)

        def at(c, shift=0):
            return velocity[c, own, pl.ds(base + shift, 8), :]

        def fy(c):
            return near_far(at(c, 1), at(c), at(c, 2), at(c, -1))

        strain_x = backward_x(outer_x(at(0)))
        strain_y = near_far(at(1), at(1, -1), at(1, 1), at(1, -2))
        strain_z = backward_z(at(2), backward)
        shear = mu[own, here, :]
        double = 2.0 * shear
        volume = lam[:, here, :] * (strain_x + strain_y + strain_z)
        change = {
            XX: volume + double * strain_x,
            YY: volume + double * strain_y,
            ZZ: volume + double * strain_z,
            XY: shear * (fy(0) + forward_x(outer_x(at(1)))),
            XZ: shear * (forward_z(at(0), forward) + forward_x(outer_x(at(2)))),
            YZ: shear * (forward_z(at(1), forward) + fy(2)),
        }
        for c, value in change.items():
            result = old[c, own, pl.ds(base, 8), :] + value
            if last:
                new[SOURCE[c], :, here, :] = result
            else:
                new[c, own, pl.ds(base, 8), :] = result

    forward_halo = {0: ((1, -FAR_COEF),), 2: ((6, FAR_COEF),), 3: ((6, NEAR_COEF), (7, FAR_COEF))}
    backward_halo = {0: ((1, -NEAR_COEF), (0, -FAR_COEF)), 1: ((1, -FAR_COEF),), 3: ((6, FAR_COEF),)}

    def weighted(field, c, terms, rows):
        total = None
        for layer, coef in terms:
            term = coef * field[c, layer, rows, :]
            total = term if total is None else total + term
        return total

    def velocity_halo(g, stress, partial, new):
        here, base = place(g)
        rows = pl.ds(base, 8)
        for c, (part, terms) in enumerate(((XX, forward_halo), (XY, backward_halo), (XZ, backward_halo))):
            for layer in range(cx):
                value = partial[c, layer, here, :]
                if layer in terms:
                    value = value + buo[layer, here, :] * weighted(stress, part, terms[layer], rows)
                new[c, low + layer, rows, :] = value

    def stress_halo(g, partial, velocity, new, last):
        here, base = place(g)
        rows = pl.ds(base, 8)

        def add(c, layer, value):
            if last:
                if value is not None:
                    new[SOURCE[c], layer, here, :] = new[SOURCE[c], layer, here, :] + value
            else:
                before = partial[c, low + layer, rows, :]
                new[c, low + layer, rows, :] = before if value is None else before + value

        for layer in range(cx):
            if layer in backward_halo:
                strain = weighted(velocity, 0, backward_halo[layer], rows)
                volume = lam[layer, here, :] * strain
                add(XX, layer, stiff[low + layer, here, :] * strain)
                add(YY, layer, volume)
                add(ZZ, layer, volume)
            else:
                for c in (XX, YY, ZZ):
                    add(c, layer, None)
            for c, part in ((XY, 1), (XZ, 2)):
                if layer in forward_halo:
                    add(c, layer, mu[low + layer, here, :] * weighted(velocity, part, forward_halo[layer], rows))
                else:
                    add(c, layer, None)
            add(YZ, layer, None)
        if last:
            return
        first, second, beneath, top = low, low + 1, high - 2, high - 1

        def complete(c, layer, coefs, part, terms):
            new[c, layer, rows, :] = partial[c, layer, rows, :] + coefs[layer, here, :] * weighted(velocity, part, terms, rows)

        complete(XX, 1, stiff, 0, ((first, FAR_COEF),))
        complete(XX, high, stiff, 0, ((top, -NEAR_COEF), (beneath, -FAR_COEF)))
        complete(XX, high + 1, stiff, 0, ((top, -FAR_COEF),))
        for c, part in ((XY, 1), (XZ, 2)):
            complete(c, 0, mu, part, ((first, FAR_COEF),))
            complete(c, 1, mu, part, ((first, NEAR_COEF), (second, FAR_COEF)))
            complete(c, high, mu, part, ((top, -FAR_COEF),))

    def each(first, last, function, *args):
        def body(g, carry):
            function(g, *args)
            return carry

        lax.fori_loop(first, last, body, 0)

    def each_edge_first(first, last, copy, function, *args):
        def body(p, carry):
            function(jnp.where(p == first, last - 1, p - 1), *args)

            @pl.when(p == first)
            def _():
                copy.start()

            return carry

        lax.fori_loop(first, last, body, 0)

    def each_edge_last(first, last, copy, function, *args):
        def body(g, carry):
            @pl.when(g == last - 1)
            def _():
                copy.wait_recv()

            function(g, *args)
            return carry

        lax.fori_loop(first, last, body, 0)

    each_edge_last(0, groups, y_s0, velocity_group, v0, s0, v0, False)
    x_v1, y_v1 = chunks(V1, v1, s0_bounds), y_copy(1, v1)
    x_sp, y_s1 = chunks(SP, sp, sp_bounds), y_copy(2, s1)
    parts = len(s0_bounds) - 1
    for i in range(parts):
        final = i == parts - 1
        arrive(x_s0[i])
        if final:
            each_edge_first(s0_bounds[i], groups, y_v1, velocity_halo, s0, v0, v1)
        else:
            each(s0_bounds[i], s0_bounds[i + 1], velocity_halo, s0, v0, v1)
        start(x_v1[i])
        if final:
            each_edge_last(sp_bounds[i], groups, y_v1, stress_group, s0, v1, sp, False)
        elif sp_bounds[i] < sp_bounds[i + 1]:
            each(sp_bounds[i], sp_bounds[i + 1], stress_group, s0, v1, sp, False)
        start(x_sp[i])

    for copy in ocean_loads:
        copy.wait()
    arrive(x_ocean)
    edge = pl.multiple_of(half * (1 - sec), 128)

    def ocean_columns(field, index):
        part = field.at[:, :, :] if len(field.shape) == 3 else field.at[:, :]
        if len(field.shape) == 3:
            a, b = part.at[:, :, pl.ds(edge, half)], part.at[:, :, ocy : ocy + half]
        else:
            a, b = part.at[:, pl.ds(edge, half)], part.at[:, ocy : ocy + half]
        return copy_to(a, b, os_sem.at[2, index], or_sem.at[2, index], device(0, True))

    y_ocean = [ocean_columns(oce, 0), ocean_columns(dep, 1), ocean_columns(wet, 2)]
    for copy in y_ocean:
        copy.start()

    lane = lax.broadcasted_iota(jnp.int32, (8, 128), 1)

    def spread(value):
        return jnp.broadcast_to(value, (8, 128))

    def lanes_of(index):
        mine = pltpu.roll(spread(loc[index : index + 1, :]), PAD, 1)
        below = pltpu.roll(spread(locn[0, index : index + 1, :]), 128 - (ocx - PAD), 1)
        above = pltpu.roll(spread(locn[1, index : index + 1, :]), PAD + ocx, 1)
        return jnp.where(lane < PAD, below, jnp.where(lane < PAD + ocx, mine, above))

    slot = lax.broadcasted_iota(jnp.int32, (8, 128), 0)
    picked = lanes_of(0).astype(jnp.int32) - tile + FAR_REACH == slot
    row[...] = jnp.where(picked, OCEAN_STEP * lanes_of(1), 0.0)

    for copy in y_ocean:
        copy.wait()
    region = oce.shape[1:]
    width = region[1]
    lanes = lax.broadcasted_iota(jnp.int32, (1, width), 1)
    beyond = lanes - ocy
    inside = (beyond < 0) | ((beyond < half // 2) & (sec == 0)) | ((beyond >= half // 2) & (sec == 1))
    rows = lax.broadcasted_iota(jnp.int32, (region[0], 1), 0)
    inside_rows = ((rows >= PAD) | has_low) & ((rows < PAD + ocx) | has_high)
    mask = inside.astype(jnp.float32) * inside_rows.astype(jnp.float32)
    wetf = wet[...].astype(jnp.float32) * mask
    vel1[3] = wetf
    oce[0] = oce[0] * mask
    HALF_STEP = 0.5 * OCEAN_STEP

    def ocean_flow(eta, u, v, first, count, out_u, out_v):
        here = pl.ds(first, count)
        middle = eta[here, :]
        w = vel1[3, here, :]
        new_u = w * (u[here, :] - HALF_STEP * (eta[pl.ds(first + 1, count), :] - eta[pl.ds(first - 1, count), :]))
        new_v = w * (v[here, :] - HALF_STEP * (pltpu.roll(middle, width - 1, 1) - pltpu.roll(middle, 1, 1)))
        out_u[here, :] = new_u
        out_v[here, :] = new_v
        flux[0, here, :] = dep[here, :] * new_u
        flux[1, here, :] = dep[here, :] * new_v

    def ocean_fall(first, count):
        along = flux[1, pl.ds(first, count), :]
        return HALF_STEP * (
            flux[0, pl.ds(first + 1, count), :] - flux[0, pl.ds(first - 1, count), :]
            + pltpu.roll(along, width - 1, 1) - pltpu.roll(along, 1, 1)
        )

    ocean_flow(oce.at[0], oce.at[1], oce.at[2], 4, ocx + 8, vel1.at[0], vel1.at[1])
    here = pl.ds(5, ocx + 6)
    rows_here = lax.broadcasted_iota(jnp.int32, (ocx + 6, 1), 0) + 5
    mask_here = inside.astype(jnp.float32) * (
        ((rows_here >= PAD) | has_low) & ((rows_here < PAD + ocx) | has_high)
    ).astype(jnp.float32)
    vel1[2, here, :] = (oce[0, here, :] - ocean_fall(5, ocx + 6)) * mask_here

    arrive(x_static)
    x_v2, y_v2 = chunks(V2, v2, v2_bounds), y_copy(3, v2)
    for i in range(parts):
        final = i == parts - 1
        arrive(x_v1[i])
        arrive(x_sp[i])
        if final:
            each_edge_first(sp_bounds[i], groups, y_s1, stress_halo, sp, v1, s1, False)
            each_edge_last(v2_bounds[i], groups, y_s1, velocity_group, v1, s1, v2, True, vel_out)
        else:
            if sp_bounds[i] < sp_bounds[i + 1]:
                each(sp_bounds[i], sp_bounds[i + 1], stress_halo, sp, v1, s1, False)
            if v2_bounds[i] < v2_bounds[i + 1]:
                each(v2_bounds[i], v2_bounds[i + 1], velocity_group, v1, s1, v2, True, vel_out)
        start(x_v2[i])
    y_v2.start()

    top = v2[2, own, rows_own, :].reshape(cx * cy, nz)
    first_lane = (lax.broadcasted_iota(jnp.int32, (8, nz), 1) == 0).astype(jnp.float32)
    patch = lax.dot_general(
        first_lane, top, (((1,), (1,)), ((), ())),
        precision=lax.Precision.HIGHEST, preferred_element_type=jnp.float32,
    )
    pat[8:16, 0:ocy] = patch
    patch_copies = []
    for other in (False, True):
        for step in range(-FAR_REACH, FAR_REACH + 1):
            if step == 0 and not other:
                continue
            index = FAR_REACH - step
            if other:
                source = pat.at[8:9, pl.ds(edge, half)]
                target = pat.at[index : index + 1, ocy : ocy + half]
            else:
                source = pat.at[8:9, 0:ocy]
                target = pat.at[index : index + 1, 0:ocy]
            copy = copy_to(source, target, ps_sem.at[int(other), index], pr_sem.at[int(other), index], device(step, other))
            back = (tile - step >= 0) & (tile - step < tiles)
            ahead = (tile + step >= 0) & (tile + step < tiles)
            patch_copies.append((copy, ahead, back))
    for copy, ahead, back in patch_copies:
        pl.when(ahead)(copy.start)
    pat[FAR_REACH : FAR_REACH + 1, 0:ocy] = patch[0:1]

    each_edge_last(0, groups, y_v2, stress_group, s1, v2, str_out, True)
    for i in range(parts):
        arrive(x_v2[i])
    each(0, groups, stress_halo, None, v2, str_out, True)

    for copy, ahead, back in patch_copies:
        pl.when(back)(copy.wait_recv)
    uplift = lax.dot_general(
        row[...], pat[0:8, :], (((0,), (0,)), ((), ())),
        precision=lax.Precision.HIGHEST, preferred_element_type=jnp.float32,
    )[0 : PAD + ocx + PAD]
    source = vel1[3] * uplift
    oce[0] = vel1[2] + source
    ocean_flow(oce.at[0], vel1.at[0], vel1.at[1], PAD - 1, ocx + 2, oce.at[1], oce.at[2])
    oce_out[0] = oce[0, orow_own, 0:ocy] - ocean_fall(PAD, ocx)[:, 0:ocy] + source[PAD : PAD + ocx, 0:ocy]
    oce_out[1:3] = oce[1:3, orow_own, 0:ocy]

    for copies in (*x_s0, x_static, x_ocean, *x_v1, *x_sp, *x_v2):
        sent(copies)
    for copy in (y_s0, y_v1, y_s1, y_v2):
        copy.wait_send()
    for copy, ahead, back in patch_copies:
        pl.when(ahead)(copy.wait_send)


def solution(mesh):
    tiles = mesh.shape["tile"]

    def shards(velocity, stresses, buoyancy, lame_first, shear_mod, ocean_state, depth_map, wet_mask, src, share):
        cx, cy, nz = buoyancy.shape
        ocx, ocy = depth_map.shape
        layers, rows = cx + 2 * LAY, cy + 2 * PAD
        region = (ocx + 2 * PAD, ocy + ocy // 2)
        hbm = pl.BlockSpec(memory_space=pltpu.HBM)
        vmem = pl.BlockSpec(memory_space=pltpu.VMEM)
        dma = pltpu.SemaphoreType.DMA
        f32 = jnp.float32
        return pl.pallas_call(
            functools.partial(kernel, tiles),
            out_shape=(
                jax.ShapeDtypeStruct(velocity.shape, f32),
                jax.ShapeDtypeStruct(stresses.shape, f32),
                jax.ShapeDtypeStruct(ocean_state.shape, f32),
            ),
            in_specs=[hbm] * 10,
            out_specs=(vmem,) * 3,
            scratch_shapes=[
                pltpu.VMEM((6, layers, rows, nz), f32),
                pltpu.VMEM((6, layers, rows, nz), f32),
                pltpu.VMEM((6, layers, rows, nz), f32),
                pltpu.VMEM(velocity.shape, f32),
                pltpu.VMEM((3, layers, rows, nz), f32),
                pltpu.VMEM((3, layers, rows, nz), f32),
                pltpu.VMEM(buoyancy.shape, f32),
                pltpu.VMEM(buoyancy.shape, f32),
                pltpu.VMEM((layers, cy, nz), f32),
                pltpu.VMEM((layers, cy, nz), f32),
                pltpu.VMEM((1, ocx), jnp.int32),
                pltpu.VMEM((1, ocx), f32),
                pltpu.VMEM((3, *region), f32),
                pltpu.VMEM(region, f32),
                pltpu.VMEM(region, jnp.int32),
                pltpu.VMEM((8, 128), f32),
                pltpu.VMEM((2, 8, 128), f32),
                pltpu.VMEM((16, region[1]), f32),
                pltpu.VMEM((8, 128), f32),
                pltpu.VMEM((2, *region), f32),
                pltpu.VMEM((4, *region), f32),
                dma((15,)),
                dma((5, len(BOUNDS) - 1, 2, 2)),
                dma((5, len(BOUNDS) - 1, 2, 2)),
                dma((4,)),
                dma((4,)),
                dma((3, 4)),
                dma((3, 4)),
                dma((2, 7)),
                dma((2, 7)),
            ],
            compiler_params=pltpu.CompilerParams(
                collective_id=0, has_side_effects=True, vmem_limit_bytes=40 * 1024 * 1024
            ),
        )(
            *(
                pltpu.with_memory_space_constraint(array, pltpu.HBM)
                for array in (
                    velocity, stresses, buoyancy, lame_first, shear_mod, ocean_state, depth_map, wet_mask,
                    src.reshape(1, ocx), share.reshape(1, ocx),
                )
            )
        )

    return jax.shard_map(
        shards,
        mesh=mesh,
        in_specs=(
            P(None, "tile", "sec", None),
            P(None, "tile", "sec", None),
            P("tile", "sec", None),
            P("tile", "sec", None),
            P("tile", "sec", None),
            P(None, "tile", "sec"),
            P("tile", "sec"),
            P("tile", "sec"),
            P("tile"),
            P("tile"),
        ),
        out_specs=(
            P(None, "tile", "sec", None),
            P(None, "tile", "sec", None),
            P(None, "tile", "sec"),
        ),
        check_vma=False,
    )
```

```python
import functools

import jax
import jax.numpy as jnp
from jax import lax
from jax.experimental import pallas as pl
from jax.experimental.pallas import tpu as pltpu
from jax.sharding import PartitionSpec as P

REACH = 2
FAR_REACH = REACH + 1
NEAR_COEF = 9.0 / 8.0
FAR_COEF = -1.0 / 24.0
TIME_STEP = 0.15
OCEAN_STEP = 0.3
MESH = pl.DeviceIdType.MESH

YY, YZ, XY, XZ, XX, ZZ = range(6)
SOURCE = (1, 5, 3, 4, 0, 2)

PAD = 8
LAY = 2
BOUNDS = (0, 4, 8)


def lane_coefs(shape):
    lane = lax.broadcasted_iota(jnp.int32, shape, len(shape) - 1)
    last = shape[-1] - 1

    def coef(value, keep):
        return jnp.where(keep, jnp.float32(value), jnp.float32(0.0))

    forward = (
        coef(NEAR_COEF, lane < last),
        coef(FAR_COEF, lane < last - 1),
        coef(-FAR_COEF, lane > 0),
    )
    backward = (
        coef(-NEAR_COEF, lane > 0),
        coef(FAR_COEF, lane < last),
        coef(-FAR_COEF, lane > 1),
    )
    return forward, backward


def forward_z(f, coefs):
    n, axis = f.shape[-1], f.ndim - 1
    one, two, back = coefs
    return (
        one * pltpu.roll(f, n - 1, axis)
        - NEAR_COEF * f
        + two * pltpu.roll(f, n - 2, axis)
        + back * pltpu.roll(f, 1, axis)
    )


def backward_z(f, coefs):
    n, axis = f.shape[-1], f.ndim - 1
    back, one, two = coefs
    return (
        NEAR_COEF * f
        + back * pltpu.roll(f, 1, axis)
        + one * pltpu.roll(f, n - 1, axis)
        + two * pltpu.roll(f, 2, axis)
    )


def kernel(
    tiles,
    vel_in, str_in, buo_in, lam_in, mu_in, oce_in, dep_in, wet_in, src_in, share_in,
    vel_out, str_out, oce_out,
    s0, sp, s1, v0, v1, v2, buo, lam, mu, stiff,
    src, share, oce, dep, wet, loc, locn, pat, row, flux, vel1,
    load_sem, row_sem, xs_sem, xr_sem, ys_sem, yr_sem, os_sem, or_sem, ps_sem, pr_sem,
):
    cx, cy, nz = buo_in.shape
    ocx, ocy = dep_in.shape
    half = ocy // 2
    tile = lax.axis_index("tile")
    sec = lax.axis_index("sec")
    has_low = tile > 0
    has_high = tile < tiles - 1
    own = pl.ds(LAY, cx)
    rows_own = pl.ds(PAD, cy)
    orow_own = pl.ds(PAD, ocx)

    def device(step, other=False):
        return {"sec": 1 - sec if other else sec, "tile": tile + step}

    loads = [
        pltpu.make_async_copy(str_in.at[SOURCE[c]], s0.at[c, own, rows_own], load_sem.at[0])
        for c in range(6)
    ]
    loads += [
        pltpu.make_async_copy(vel_in, v0, load_sem.at[0]),
        pltpu.make_async_copy(buo_in, buo, load_sem.at[0]),
        pltpu.make_async_copy(lam_in, lam, load_sem.at[0]),
        pltpu.make_async_copy(mu_in, mu.at[own], load_sem.at[0]),
    ]
    ocean_loads = [
        pltpu.make_async_copy(oce_in, oce.at[:, orow_own, 0:ocy], load_sem.at[1]),
        pltpu.make_async_copy(dep_in, dep.at[orow_own, 0:ocy], load_sem.at[1]),
        pltpu.make_async_copy(wet_in, wet.at[orow_own, 0:ocy], load_sem.at[1]),
    ]
    row_loads = [
        pltpu.make_async_copy(src_in, src, row_sem.at[0]),
        pltpu.make_async_copy(share_in, share, row_sem.at[1]),
    ]

    def wait_for(sem, *sizes):
        part = s0.at[tuple(pl.ds(0, size) for size in sizes)]
        pltpu.make_async_copy(part, part, sem).wait()

    pat[...] = jnp.zeros(pat.shape, jnp.float32)

    barrier = pltpu.get_barrier_semaphore()
    pl.semaphore_signal(barrier, inc=1, device_id=device(0, True), device_id_type=MESH)

    @pl.when(has_low)
    def _():
        pl.semaphore_signal(barrier, inc=1, device_id=device(-1), device_id_type=MESH)

    @pl.when(has_high)
    def _():
        pl.semaphore_signal(barrier, inc=1, device_id=device(1), device_id_type=MESH)

    pl.semaphore_wait(barrier, 1 + has_low.astype(jnp.int32) + has_high.astype(jnp.int32))

    def copy_to(source, target, send, receive, where):
        return pltpu.make_async_remote_copy(
            src_ref=source, dst_ref=target, send_sem=send, recv_sem=receive,
            device_id=where, device_id_type=MESH,
        )

    low, high = LAY, LAY + cx
    groups = cy // 8

    def bounds_after(bounds):
        return [0] + [max(b - 1, 0) for b in bounds[1:-1]] + [groups]

    s0_bounds = list(BOUNDS)
    sp_bounds = bounds_after(s0_bounds)
    v2_bounds = bounds_after(sp_bounds)

    def rows_of(first, last):
        return pl.multiple_of(8 * first + sec * (cy - 8 * first - 8 * last), 8), 8 * (last - first)

    S0, V1, SP, V2, STATIC = range(5)
    LAYERS = ((5, 4), (4, 5), (5, 4), (4, 5), (3, 3))

    def x_copies(number, field, chunk=0, first=0, last=groups, source=None):
        if first == last:
            return [], [], 0, None
        begin, count = rows_of(first, last)
        rows = pl.ds(PAD + begin, count)
        if number in (S0, SP):
            if source is None:
                near, far = field.at[XX, :, rows], field.at[XY : XZ + 1, :, rows]
                shift = 0
            else:
                near = source.at[SOURCE[XX], :, pl.ds(begin, count)]
                far = source.at[SOURCE[XY] : SOURCE[XZ] + 1, :, pl.ds(begin, count)]
                shift = LAY
            ups = [
                (near.at[high - 1 - shift : high - shift], field.at[XX, 1:2, rows]),
                (far.at[:, high - 2 - shift : high - shift], field.at[XY : XZ + 1, 0:2, rows]),
            ]
            downs = [
                (near.at[low - shift : low + 2 - shift], field.at[XX, high : high + 2, rows]),
                (far.at[:, low - shift : low + 1 - shift], field.at[XY : XZ + 1, high : high + 1, rows]),
            ]
        elif number in (V1, V2):
            near, far = field.at[0, :, rows], field.at[1:3, :, rows]
            ups = [
                (near.at[high - 2 : high], field.at[0, 0:2, rows]),
                (far.at[:, high - 1 : high], field.at[1:3, 1:2, rows]),
            ]
            downs = [
                (near.at[low : low + 1], field.at[0, high : high + 1, rows]),
                (far.at[:, low : low + 2], field.at[1:3, high : high + 2, rows]),
            ]
        else:
            ups = [(stiff.at[high - 1 : high], stiff.at[1:2]), (mu.at[high - 2 : high], mu.at[0:2])]
            downs = [(stiff.at[low : low + 2], stiff.at[high : high + 2]), (mu.at[low : low + 1], mu.at[high : high + 1])]
        up = [
            copy_to(a, b, xs_sem.at[0], xr_sem.at[number, chunk, 0], device(1))
            for a, b in ups
        ]
        down = [
            copy_to(a, b, xs_sem.at[1], xr_sem.at[number, chunk, 1], device(-1))
            for a, b in downs
        ]
        return up, down, count, [xr_sem.at[number, chunk, d] for d in range(2)] + [LAYERS[number]]

    def chunks(number, field, bounds, source=None):
        return [
            x_copies(number, field, i, first, last, source)
            for i, (first, last) in enumerate(zip(bounds[:-1], bounds[1:]))
        ]

    def start(copies):
        up, down = copies[:2]

        @pl.when(has_high)
        def _():
            for copy in up:
                copy.start()

        @pl.when(has_low)
        def _():
            for copy in down:
                copy.start()

    def arrive(copies):
        count = copies[2]
        if count == 0:
            return
        from_low, from_high, layers = copies[3]

        @pl.when(has_low)
        def _():
            wait_for(from_low, 1, layers[0], count)

        @pl.when(has_high)
        def _():
            wait_for(from_high, 1, layers[1], count)

    def ocean_wait(sem):
        wait_for(sem, 1, 2, (5 * PAD * ocy // nz + 2 * PAD) // 2)

    y_from = pl.multiple_of(cy - (cy - PAD) * sec, 8)
    y_to = pl.multiple_of((cy + PAD) * sec, 8)

    def y_copy(number, field):
        part = field.at[0:3, own]
        return copy_to(
            part.at[:, :, pl.ds(y_from, PAD)],
            part.at[:, :, pl.ds(y_to, PAD)],
            ys_sem.at[0], yr_sem.at[number], device(0, True),
        )

    x_s0 = chunks(S0, s0, s0_bounds, str_in)
    for part in x_s0:
        start(part)
    for copy in row_loads + loads + ocean_loads:
        copy.start()

    outer = pl.multiple_of((cy + PAD) * sec, 8)
    for field in (s0, s1):
        field[0:3, own, pl.ds(outer, PAD), :] = jnp.zeros((3, cx, PAD, nz), jnp.float32)
    for field in (v1, v2):
        field[:, own, pl.ds(outer, PAD), :] = jnp.zeros((3, cx, PAD, nz), jnp.float32)

    def clear(layers, orow, slot):
        for field in (s0, sp):
            field[XY : XX + 1, layers, rows_own, :] = jnp.zeros((3, LAY, cy, nz), jnp.float32)
        for field in (v1, v2):
            field[:, layers, rows_own, :] = jnp.zeros((3, LAY, cy, nz), jnp.float32)
        for field in (mu, stiff):
            field[layers] = jnp.zeros((LAY, cy, nz), jnp.float32)
        oce[:, orow, 0:ocy] = jnp.zeros((3, PAD, ocy), jnp.float32)
        dep[orow, 0:ocy] = jnp.zeros((PAD, ocy), jnp.float32)
        wet[orow, 0:ocy] = jnp.zeros((PAD, ocy), jnp.int32)
        locn[slot] = jnp.zeros(locn.shape[1:], jnp.float32)

    @pl.when(jnp.logical_not(has_low))
    def _():
        clear(slice(0, LAY), slice(0, PAD), 0)

    @pl.when(jnp.logical_not(has_high))
    def _():
        clear(slice(LAY + cx, LAY + cx + LAY), slice(PAD + ocx, PAD + ocx + PAD), 1)

    loc[...] = jnp.zeros(loc.shape, jnp.float32)
    for copy in row_loads:
        copy.wait()
    loc[0:1, 0:ocx] = src[...].astype(jnp.float32)
    loc[1:2, 0:ocx] = share[...]

    def ocean_rows(step, first, target, slot, index):
        return [
            copy_to(oce_in.at[:, pl.ds(first, PAD)], oce.at[:, pl.ds(target, PAD), 0:ocy], os_sem.at[index], or_sem.at[index], device(step)),
            copy_to(dep_in.at[pl.ds(first, PAD)], dep.at[pl.ds(target, PAD), 0:ocy], os_sem.at[index], or_sem.at[index], device(step)),
            copy_to(wet_in.at[pl.ds(first, PAD)], wet.at[pl.ds(target, PAD), 0:ocy], os_sem.at[index], or_sem.at[index], device(step)),
            copy_to(loc, locn.at[slot], os_sem.at[index], or_sem.at[index], device(step)),
        ]

    x_ocean = (
        ocean_rows(1, ocx - PAD, 0, 0, 0),
        ocean_rows(-1, 0, PAD + ocx, 1, 1),
    )
    wait_for(load_sem.at[0], 6, 2 * cx, cy)
    y_s0 = y_copy(0, s0)
    y_s0.start()

    buo[...] = TIME_STEP * buo[...]
    lam[...] = TIME_STEP * lam[...]
    mu[own] = TIME_STEP * mu[own]
    stiff[own] = lam[...] + 2.0 * mu[own]
    x_static = x_copies(STATIC, None)
    start(x_static)
    start(x_ocean)

    forward, backward = lane_coefs((1, 1, nz))

    def near_far(a, b, c, d):
        return NEAR_COEF * (a - b) + FAR_COEF * (c - d)

    def outer_x(a):
        zero = jnp.zeros_like(a[0:1])
        return jnp.concatenate([zero, zero, a, zero, zero])

    def forward_x(a):
        return near_far(a[3 : 3 + cx], a[2 : 2 + cx], a[4 : 4 + cx], a[1 : 1 + cx])

    def backward_x(a):
        return near_far(a[2 : 2 + cx], a[1 : 1 + cx], a[3 : 3 + cx], a[0:cx])

    every = pl.ds(0, cx + 2 * LAY)

    def place(g):
        begin = pl.multiple_of(8 * (g + sec * (groups - 1 - 2 * g)), 8)
        return pl.ds(begin, 8), begin + PAD

    def velocity_group(g, old, stress, new, halos, out=None):
        here, base = place(g)

        def at(c, layers=own, shift=0):
            return stress[c, layers, pl.ds(base + shift, 8), :]

        def fy(c):
            return near_far(at(c, own, 1), at(c), at(c, own, 2), at(c, own, -1))

        def by(c):
            return near_far(at(c), at(c, own, -1), at(c, own, 1), at(c, own, -2))

        def wide(c):
            return at(c, every) if halos else outer_x(at(c))

        scale = buo[:, here, :]
        x = forward_x(wide(XX)) + by(XY) + backward_z(at(XZ), backward)
        y = backward_x(wide(XY)) + fy(YY) + backward_z(at(YZ), backward)
        z = backward_x(wide(XZ)) + by(YZ) + forward_z(at(ZZ), forward)
        for c, value in enumerate((x, y, z)):
            if halos:
                result = old[c, own, pl.ds(base, 8), :] + scale * value
                new[c, own, pl.ds(base, 8), :] = result
                out[c, :, here, :] = result
            else:
                new[c, :, here, :] = old[c, :, here, :] + scale * value

    def stress_group(g, old, velocity, new, last):
        here, base = place(g)

        def at(c, shift=0):
            return velocity[c, own, pl.ds(base + shift, 8), :]

        def fy(c):
            return near_far(at(c, 1), at(c), at(c, 2), at(c, -1))

        strain_x = backward_x(outer_x(at(0)))
        strain_y = near_far(at(1), at(1, -1), at(1, 1), at(1, -2))
        strain_z = backward_z(at(2), backward)
        shear = mu[own, here, :]
        double = 2.0 * shear
        volume = lam[:, here, :] * (strain_x + strain_y + strain_z)
        change = {
            XX: volume + double * strain_x,
            YY: volume + double * strain_y,
            ZZ: volume + double * strain_z,
            XY: shear * (fy(0) + forward_x(outer_x(at(1)))),
            XZ: shear * (forward_z(at(0), forward) + forward_x(outer_x(at(2)))),
            YZ: shear * (forward_z(at(1), forward) + fy(2)),
        }
        for c, value in change.items():
            result = old[c, own, pl.ds(base, 8), :] + value
            if last:
                new[SOURCE[c], :, here, :] = result
            else:
                new[c, own, pl.ds(base, 8), :] = result

    forward_halo = {0: ((1, -FAR_COEF),), 2: ((6, FAR_COEF),), 3: ((6, NEAR_COEF), (7, FAR_COEF))}
    backward_halo = {0: ((1, -NEAR_COEF), (0, -FAR_COEF)), 1: ((1, -FAR_COEF),), 3: ((6, FAR_COEF),)}

    def weighted(field, c, terms, rows):
        total = None
        for layer, coef in terms:
            term = coef * field[c, layer, rows, :]
            total = term if total is None else total + term
        return total

    def velocity_halo(g, stress, partial, new):
        here, base = place(g)
        rows = pl.ds(base, 8)
        for c, (part, terms) in enumerate(((XX, forward_halo), (XY, backward_halo), (XZ, backward_halo))):
            for layer in range(cx):
                value = partial[c, layer, here, :]
                if layer in terms:
                    value = value + buo[layer, here, :] * weighted(stress, part, terms[layer], rows)
                new[c, low + layer, rows, :] = value

    def stress_halo(g, partial, velocity, new, last):
        here, base = place(g)
        rows = pl.ds(base, 8)

        def add(c, layer, value):
            if last:
                if value is not None:
                    new[SOURCE[c], layer, here, :] = new[SOURCE[c], layer, here, :] + value
            else:
                before = partial[c, low + layer, rows, :]
                new[c, low + layer, rows, :] = before if value is None else before + value

        for layer in range(cx):
            if layer in backward_halo:
                strain = weighted(velocity, 0, backward_halo[layer], rows)
                volume = lam[layer, here, :] * strain
                add(XX, layer, stiff[low + layer, here, :] * strain)
                add(YY, layer, volume)
                add(ZZ, layer, volume)
            else:
                for c in (XX, YY, ZZ):
                    add(c, layer, None)
            for c, part in ((XY, 1), (XZ, 2)):
                if layer in forward_halo:
                    add(c, layer, mu[low + layer, here, :] * weighted(velocity, part, forward_halo[layer], rows))
                else:
                    add(c, layer, None)
            add(YZ, layer, None)
        if last:
            return
        first, second, beneath, top = low, low + 1, high - 2, high - 1

        def complete(c, layer, coefs, part, terms):
            new[c, layer, rows, :] = partial[c, layer, rows, :] + coefs[layer, here, :] * weighted(velocity, part, terms, rows)

        complete(XX, 1, stiff, 0, ((first, FAR_COEF),))
        complete(XX, high, stiff, 0, ((top, -NEAR_COEF), (beneath, -FAR_COEF)))
        complete(XX, high + 1, stiff, 0, ((top, -FAR_COEF),))
        for c, part in ((XY, 1), (XZ, 2)):
            complete(c, 0, mu, part, ((first, FAR_COEF),))
            complete(c, 1, mu, part, ((first, NEAR_COEF), (second, FAR_COEF)))
            complete(c, high, mu, part, ((top, -FAR_COEF),))

    def each(first, last, function, *args):
        def body(g, carry):
            function(g, *args)
            return carry

        lax.fori_loop(first, last, body, 0)

    def each_edge_first(first, last, copy, function, *args):
        def body(p, carry):
            function(jnp.where(p == first, last - 1, p - 1), *args)

            @pl.when(p == first)
            def _():
                copy.start()

            return carry

        lax.fori_loop(first, last, body, 0)

    def each_edge_last(first, last, copy, function, *args):
        def body(g, carry):
            @pl.when(g == last - 1)
            def _():
                copy.wait_recv()

            function(g, *args)
            return carry

        lax.fori_loop(first, last, body, 0)

    each_edge_last(0, groups, y_s0, velocity_group, v0, s0, v0, False)
    x_v1, y_v1 = chunks(V1, v1, s0_bounds), y_copy(1, v1)
    x_sp, y_s1 = chunks(SP, sp, sp_bounds), y_copy(2, s1)
    parts = len(s0_bounds) - 1
    for i in range(parts):
        final = i == parts - 1
        arrive(x_s0[i])
        if final:
            each_edge_first(s0_bounds[i], groups, y_v1, velocity_halo, s0, v0, v1)
        else:
            each(s0_bounds[i], s0_bounds[i + 1], velocity_halo, s0, v0, v1)
        start(x_v1[i])
        if final:
            each_edge_last(sp_bounds[i], groups, y_v1, stress_group, s0, v1, sp, False)
        elif sp_bounds[i] < sp_bounds[i + 1]:
            each(sp_bounds[i], sp_bounds[i + 1], stress_group, s0, v1, sp, False)
        start(x_sp[i])

    wait_for(load_sem.at[1], 5, ocx * ocy // (nz * cy), cy)
    pl.when(has_low)(lambda: ocean_wait(or_sem.at[0]))
    pl.when(has_high)(lambda: ocean_wait(or_sem.at[1]))
    edge = pl.multiple_of(half * (1 - sec), 128)

    def ocean_columns(field):
        where = (slice(None),) * (len(field.shape) - 1)
        a, b = field.at[(*where, pl.ds(edge, half))], field.at[(*where, pl.ds(ocy, half))]
        return copy_to(a, b, os_sem.at[2], or_sem.at[2], device(0, True))

    y_ocean = [ocean_columns(oce), ocean_columns(dep), ocean_columns(wet)]
    for copy in y_ocean:
        copy.start()

    lane = lax.broadcasted_iota(jnp.int32, (8, 128), 1)

    def spread(value):
        return jnp.broadcast_to(value, (8, 128))

    def lanes_of(index):
        mine = pltpu.roll(spread(loc[index : index + 1, :]), PAD, 1)
        below = pltpu.roll(spread(locn[0, index : index + 1, :]), 128 - (ocx - PAD), 1)
        above = pltpu.roll(spread(locn[1, index : index + 1, :]), PAD + ocx, 1)
        return jnp.where(lane < PAD, below, jnp.where(lane < PAD + ocx, mine, above))

    slot = lax.broadcasted_iota(jnp.int32, (8, 128), 0)
    picked = lanes_of(0).astype(jnp.int32) - tile + FAR_REACH == slot
    row[...] = jnp.where(picked, OCEAN_STEP * lanes_of(1), 0.0)

    for sem in (or_sem.at[2], os_sem.at[2]):
        wait_for(sem, 1, 5, ocx + 2 * PAD)
    region = oce.shape[1:]
    width = region[1]
    lanes = lax.broadcasted_iota(jnp.int32, (1, width), 1)
    beyond = lanes - ocy
    inside = (beyond < 0) | ((beyond < half // 2) & (sec == 0)) | ((beyond >= half // 2) & (sec == 1))
    rows = lax.broadcasted_iota(jnp.int32, (region[0], 1), 0)
    inside_rows = ((rows >= PAD) | has_low) & ((rows < PAD + ocx) | has_high)
    mask = inside.astype(jnp.float32) * inside_rows.astype(jnp.float32)
    wetf = wet[...].astype(jnp.float32) * mask
    vel1[3] = wetf
    oce[0] = oce[0] * mask
    HALF_STEP = 0.5 * OCEAN_STEP

    def ocean_flow(eta, u, v, first, count, out_u, out_v):
        here = pl.ds(first, count)
        middle = eta[here, :]
        w = vel1[3, here, :]
        new_u = w * (u[here, :] - HALF_STEP * (eta[pl.ds(first + 1, count), :] - eta[pl.ds(first - 1, count), :]))
        new_v = w * (v[here, :] - HALF_STEP * (pltpu.roll(middle, width - 1, 1) - pltpu.roll(middle, 1, 1)))
        out_u[here, :] = new_u
        out_v[here, :] = new_v
        flux[0, here, :] = dep[here, :] * new_u
        flux[1, here, :] = dep[here, :] * new_v

    def ocean_fall(first, count):
        along = flux[1, pl.ds(first, count), :]
        return HALF_STEP * (
            flux[0, pl.ds(first + 1, count), :] - flux[0, pl.ds(first - 1, count), :]
            + pltpu.roll(along, width - 1, 1) - pltpu.roll(along, 1, 1)
        )

    ocean_flow(oce.at[0], oce.at[1], oce.at[2], 4, ocx + 8, vel1.at[0], vel1.at[1])
    here = pl.ds(5, ocx + 6)
    rows_here = lax.broadcasted_iota(jnp.int32, (ocx + 6, 1), 0) + 5
    mask_here = inside.astype(jnp.float32) * (
        ((rows_here >= PAD) | has_low) & ((rows_here < PAD + ocx) | has_high)
    ).astype(jnp.float32)
    vel1[2, here, :] = (oce[0, here, :] - ocean_fall(5, ocx + 6)) * mask_here

    arrive(x_static)
    x_v2, y_v2 = chunks(V2, v2, v2_bounds), y_copy(3, v2)
    for i in range(parts):
        final = i == parts - 1
        arrive(x_v1[i])
        arrive(x_sp[i])
        if final:
            each_edge_first(sp_bounds[i], groups, y_s1, stress_halo, sp, v1, s1, False)
            each_edge_last(v2_bounds[i], groups, y_s1, velocity_group, v1, s1, v2, True, vel_out)
        else:
            if sp_bounds[i] < sp_bounds[i + 1]:
                each(sp_bounds[i], sp_bounds[i + 1], stress_halo, sp, v1, s1, False)
            if v2_bounds[i] < v2_bounds[i + 1]:
                each(v2_bounds[i], v2_bounds[i + 1], velocity_group, v1, s1, v2, True, vel_out)
        start(x_v2[i])
    y_v2.start()

    top = v2[2, own, rows_own, :].reshape(cx * cy, nz)
    first_lane = (lax.broadcasted_iota(jnp.int32, (8, nz), 1) == 0).astype(jnp.float32)
    patch = lax.dot_general(
        first_lane, top, (((1,), (1,)), ((), ())),
        precision=lax.Precision.HIGHEST, preferred_element_type=jnp.float32,
    )
    pat[8:16, 0:ocy] = patch
    patch_copies = []
    for other in (False, True):
        for step in range(-FAR_REACH, FAR_REACH + 1):
            if step == 0 and not other:
                continue
            index = FAR_REACH - step
            if other:
                source = pat.at[8:9, pl.ds(edge, half)]
                target = pat.at[index : index + 1, ocy : ocy + half]
            else:
                source = pat.at[8:9, 0:ocy]
                target = pat.at[index : index + 1, 0:ocy]
            copy = copy_to(source, target, ps_sem.at[int(other), index], pr_sem.at[int(other), index], device(step, other))
            back = (tile - step >= 0) & (tile - step < tiles)
            ahead = (tile + step >= 0) & (tile + step < tiles)
            patch_copies.append((copy, ahead, back))
    for copy, ahead, back in patch_copies:
        pl.when(ahead)(copy.start)
    pat[FAR_REACH : FAR_REACH + 1, 0:ocy] = patch[0:1]

    each_edge_last(0, groups, y_v2, stress_group, s1, v2, str_out, True)
    for i in range(parts):
        arrive(x_v2[i])
    each(0, groups, stress_halo, None, v2, str_out, True)

    for copy, ahead, back in patch_copies:
        pl.when(back)(copy.wait_recv)
    uplift = lax.dot_general(
        row[...], pat[0:8, :], (((0,), (0,)), ((), ())),
        precision=lax.Precision.HIGHEST, preferred_element_type=jnp.float32,
    )[0 : PAD + ocx + PAD]
    source = vel1[3] * uplift
    oce[0] = vel1[2] + source
    ocean_flow(oce.at[0], vel1.at[0], vel1.at[1], PAD - 1, ocx + 2, oce.at[1], oce.at[2])
    oce_out[0] = oce[0, orow_own, 0:ocy] - ocean_fall(PAD, ocx)[:, 0:ocy] + source[PAD : PAD + ocx, 0:ocy]
    oce_out[1:3] = oce[1:3, orow_own, 0:ocy]

    @pl.when(has_high)
    def _():
        wait_for(xs_sem.at[0], 3, 7, cy)
        ocean_wait(os_sem.at[0])

    @pl.when(has_low)
    def _():
        wait_for(xs_sem.at[1], 3, 7, cy)
        ocean_wait(os_sem.at[1])

    wait_for(ys_sem.at[0], 6, 8, 2 * cx)
    for copy, ahead, back in patch_copies:
        pl.when(ahead)(copy.wait_send)


def store(velocity, stresses, ocean, vel_out, str_out, oce_out, sem):
    copies = [
        pltpu.make_async_copy(a, b, sem.at[i])
        for i, (a, b) in enumerate(((stresses, str_out), (velocity, vel_out), (ocean, oce_out)))
    ]
    for copy in copies:
        copy.start()
    for copy in copies:
        copy.wait()


def solution(mesh):
    tiles = mesh.shape["tile"]

    def shards(velocity, stresses, buoyancy, lame_first, shear_mod, ocean_state, depth_map, wet_mask, src, share):
        cx, cy, nz = buoyancy.shape
        ocx, ocy = depth_map.shape
        layers, rows = cx + 2 * LAY, cy + 2 * PAD
        region = (ocx + 2 * PAD, ocy + ocy // 2)
        hbm = pl.BlockSpec(memory_space=pltpu.HBM)
        vmem = pl.BlockSpec(memory_space=pltpu.VMEM)
        dma = pltpu.SemaphoreType.DMA
        f32 = jnp.float32
        results = pl.pallas_call(
            functools.partial(kernel, tiles),
            out_shape=(
                jax.ShapeDtypeStruct(velocity.shape, f32),
                jax.ShapeDtypeStruct(stresses.shape, f32),
                jax.ShapeDtypeStruct(ocean_state.shape, f32),
            ),
            in_specs=[hbm] * 10,
            out_specs=(vmem,) * 3,
            scratch_shapes=[
                pltpu.VMEM((6, layers, rows, nz), f32),
                pltpu.VMEM((6, layers, rows, nz), f32),
                pltpu.VMEM((6, layers, rows, nz), f32),
                pltpu.VMEM(velocity.shape, f32),
                pltpu.VMEM((3, layers, rows, nz), f32),
                pltpu.VMEM((3, layers, rows, nz), f32),
                pltpu.VMEM(buoyancy.shape, f32),
                pltpu.VMEM(buoyancy.shape, f32),
                pltpu.VMEM((layers, cy, nz), f32),
                pltpu.VMEM((layers, cy, nz), f32),
                pltpu.VMEM((1, ocx), jnp.int32),
                pltpu.VMEM((1, ocx), f32),
                pltpu.VMEM((3, *region), f32),
                pltpu.VMEM(region, f32),
                pltpu.VMEM(region, jnp.int32),
                pltpu.VMEM((2 * PAD, 128), f32),
                pltpu.VMEM((2, 2 * PAD, 128), f32),
                pltpu.VMEM((16, region[1]), f32),
                pltpu.VMEM((8, 128), f32),
                pltpu.VMEM((2, *region), f32),
                pltpu.VMEM((4, *region), f32),
                dma((2,)),
                dma((2,)),
                dma((2,)),
                dma((5, len(BOUNDS) - 1, 2)),
                dma((1,)),
                dma((4,)),
                dma((3,)),
                dma((3,)),
                dma((2, 7)),
                dma((2, 7)),
            ],
            compiler_params=pltpu.CompilerParams(
                collective_id=0, has_side_effects=True, vmem_limit_bytes=40 * 1024 * 1024
            ),
        )(
            *(
                pltpu.with_memory_space_constraint(array, pltpu.HBM)
                for array in (
                    velocity, stresses, buoyancy, lame_first, shear_mod, ocean_state, depth_map, wet_mask,
                    src.reshape(1, ocx), share.reshape(1, ocx),
                )
            )
        )
        return pl.pallas_call(
            store,
            out_shape=tuple(jax.ShapeDtypeStruct(r.shape, f32) for r in results),
            in_specs=[vmem] * 3,
            out_specs=(hbm,) * 3,
            scratch_shapes=[dma((3,))],
            compiler_params=pltpu.CompilerParams(vmem_limit_bytes=8 * 1024 * 1024),
        )(*results)

    return jax.shard_map(
        shards,
        mesh=mesh,
        in_specs=(
            P(None, "tile", "sec", None),
            P(None, "tile", "sec", None),
            P("tile", "sec", None),
            P("tile", "sec", None),
            P("tile", "sec", None),
            P(None, "tile", "sec"),
            P("tile", "sec"),
            P("tile", "sec"),
            P("tile"),
            P("tile"),
        ),
        out_specs=(
            P(None, "tile", "sec", None),
            P(None, "tile", "sec", None),
            P(None, "tile", "sec"),
        ),
        check_vma=False,
    )
```

```python
import functools

import jax
import jax.numpy as jnp
from jax import lax
from jax.experimental import pallas as pl
from jax.experimental.pallas import tpu as pltpu
from jax.sharding import PartitionSpec as P

REACH = 2
FAR_REACH = REACH + 1
NEAR_COEF = 9.0 / 8.0
FAR_COEF = -1.0 / 24.0
TIME_STEP = 0.15
OCEAN_STEP = 0.3
MESH = pl.DeviceIdType.MESH

YY, YZ, XY, XZ, XX, ZZ = range(6)
SOURCE = (1, 5, 3, 4, 0, 2)

PAD = 8
LAY = 2
BOUNDS = (0, 7, 8)


def lane_coefs(shape):
    lane = lax.broadcasted_iota(jnp.int32, shape, len(shape) - 1)
    last = shape[-1] - 1

    def coef(value, keep):
        return jnp.where(keep, jnp.float32(value), jnp.float32(0.0))

    forward = (
        coef(NEAR_COEF, lane < last),
        coef(FAR_COEF, lane < last - 1),
        coef(-FAR_COEF, lane > 0),
    )
    backward = (
        coef(-NEAR_COEF, lane > 0),
        coef(FAR_COEF, lane < last),
        coef(-FAR_COEF, lane > 1),
    )
    return forward, backward


def forward_z(f, coefs):
    n, axis = f.shape[-1], f.ndim - 1
    one, two, back = coefs
    return (
        one * pltpu.roll(f, n - 1, axis)
        - NEAR_COEF * f
        + two * pltpu.roll(f, n - 2, axis)
        + back * pltpu.roll(f, 1, axis)
    )


def backward_z(f, coefs):
    n, axis = f.shape[-1], f.ndim - 1
    back, one, two = coefs
    return (
        NEAR_COEF * f
        + back * pltpu.roll(f, 1, axis)
        + one * pltpu.roll(f, n - 1, axis)
        + two * pltpu.roll(f, 2, axis)
    )


def kernel(
    tiles,
    vel_in, str_in, buo_in, lam_in, mu_in, oce_in, dep_in, wet_in, src_in, share_in,
    vel_out, str_out, oce_out,
    s0, sp, s1, v0, v1, v2, buo, lam, mu, stiff,
    src, share, oce, dep, wet, loc, locn, pat, row, flux, vel1,
    load_sem, row_sem, xs_sem, xr_sem, ys_sem, yr_sem, os_sem, or_sem, ps_sem, pr_sem,
):
    cx, cy, nz = buo_in.shape
    ocx, ocy = dep_in.shape
    half = ocy // 2
    tile = lax.axis_index("tile")
    sec = lax.axis_index("sec")
    has_low = tile > 0
    has_high = tile < tiles - 1
    own = pl.ds(LAY, cx)
    rows_own = pl.ds(PAD, cy)
    orow_own = pl.ds(PAD, ocx)

    def device(step, other=False):
        return {"sec": 1 - sec if other else sec, "tile": tile + step}

    loads = [
        pltpu.make_async_copy(str_in.at[SOURCE[c]], s0.at[c, own, rows_own], load_sem.at[0])
        for c in range(6)
    ]
    loads += [
        pltpu.make_async_copy(vel_in, v0, load_sem.at[0]),
        pltpu.make_async_copy(buo_in, buo, load_sem.at[0]),
        pltpu.make_async_copy(lam_in, lam, load_sem.at[0]),
        pltpu.make_async_copy(mu_in, mu.at[own], load_sem.at[0]),
    ]
    ocean_loads = [
        pltpu.make_async_copy(oce_in, oce.at[:, orow_own, 0:ocy], load_sem.at[1]),
        pltpu.make_async_copy(dep_in, dep.at[orow_own, 0:ocy], load_sem.at[1]),
        pltpu.make_async_copy(wet_in, wet.at[orow_own, 0:ocy], load_sem.at[1]),
    ]
    row_loads = [
        pltpu.make_async_copy(src_in, src, row_sem.at[0]),
        pltpu.make_async_copy(share_in, share, row_sem.at[1]),
    ]

    def wait_for(sem, *sizes):
        part = s0.at[tuple(pl.ds(0, size) for size in sizes)]
        pltpu.make_async_copy(part, part, sem).wait()

    pat[...] = jnp.zeros(pat.shape, jnp.float32)

    barrier = pltpu.get_barrier_semaphore()
    pl.semaphore_signal(barrier, inc=1, device_id=device(0, True), device_id_type=MESH)

    @pl.when(has_low)
    def _():
        pl.semaphore_signal(barrier, inc=1, device_id=device(-1), device_id_type=MESH)

    @pl.when(has_high)
    def _():
        pl.semaphore_signal(barrier, inc=1, device_id=device(1), device_id_type=MESH)

    pl.semaphore_wait(barrier, 1 + has_low.astype(jnp.int32) + has_high.astype(jnp.int32))

    def copy_to(source, target, send, receive, where):
        return pltpu.make_async_remote_copy(
            src_ref=source, dst_ref=target, send_sem=send, recv_sem=receive,
            device_id=where, device_id_type=MESH,
        )

    low, high = LAY, LAY + cx
    groups = cy // 8

    def bounds_after(bounds):
        return [0] + [max(b - 1, 0) for b in bounds[1:-1]] + [groups]

    s0_bounds = list(BOUNDS)
    sp_bounds = bounds_after(s0_bounds)
    v2_bounds = bounds_after(sp_bounds)

    def rows_of(first, last):
        return pl.multiple_of(8 * first + sec * (cy - 8 * first - 8 * last), 8), 8 * (last - first)

    S0, V1, SP, V2, STATIC = range(5)
    LAYERS = ((5, 4), (4, 5), (5, 4), (4, 5), (3, 3))

    def x_copies(number, field, chunk=0, first=0, last=groups, source=None):
        if first == last:
            return [], [], 0, None
        begin, count = rows_of(first, last)
        rows = pl.ds(PAD + begin, count)
        if number in (S0, SP):
            if source is None:
                near, far = field.at[XX, :, rows], field.at[XY : XZ + 1, :, rows]
                shift = 0
            else:
                near = source.at[SOURCE[XX], :, pl.ds(begin, count)]
                far = source.at[SOURCE[XY] : SOURCE[XZ] + 1, :, pl.ds(begin, count)]
                shift = LAY
            ups = [
                (near.at[high - 1 - shift : high - shift], field.at[XX, 1:2, rows]),
                (far.at[:, high - 2 - shift : high - shift], field.at[XY : XZ + 1, 0:2, rows]),
            ]
            downs = [
                (near.at[low - shift : low + 2 - shift], field.at[XX, high : high + 2, rows]),
                (far.at[:, low - shift : low + 1 - shift], field.at[XY : XZ + 1, high : high + 1, rows]),
            ]
        elif number in (V1, V2):
            near, far = field.at[0, :, rows], field.at[1:3, :, rows]
            ups = [
                (near.at[high - 2 : high], field.at[0, 0:2, rows]),
                (far.at[:, high - 1 : high], field.at[1:3, 1:2, rows]),
            ]
            downs = [
                (near.at[low : low + 1], field.at[0, high : high + 1, rows]),
                (far.at[:, low : low + 2], field.at[1:3, high : high + 2, rows]),
            ]
        else:
            ups = [(stiff.at[high - 1 : high], stiff.at[1:2]), (mu.at[high - 2 : high], mu.at[0:2])]
            downs = [(stiff.at[low : low + 2], stiff.at[high : high + 2]), (mu.at[low : low + 1], mu.at[high : high + 1])]
        up = [
            copy_to(a, b, xs_sem.at[0], xr_sem.at[number, chunk, 0], device(1))
            for a, b in ups
        ]
        down = [
            copy_to(a, b, xs_sem.at[1], xr_sem.at[number, chunk, 1], device(-1))
            for a, b in downs
        ]
        return up, down, count, [xr_sem.at[number, chunk, d] for d in range(2)] + [LAYERS[number]]

    def chunks(number, field, bounds, source=None):
        return [
            x_copies(number, field, i, first, last, source)
            for i, (first, last) in enumerate(zip(bounds[:-1], bounds[1:]))
        ]

    def start(copies):
        up, down = copies[:2]

        @pl.when(has_high)
        def _():
            for copy in up:
                copy.start()

        @pl.when(has_low)
        def _():
            for copy in down:
                copy.start()

    def arrive(copies):
        count = copies[2]
        if count == 0:
            return
        from_low, from_high, layers = copies[3]

        @pl.when(has_low)
        def _():
            wait_for(from_low, 1, layers[0], count)

        @pl.when(has_high)
        def _():
            wait_for(from_high, 1, layers[1], count)

    def ocean_wait(sem):
        wait_for(sem, 1, 2, (5 * PAD * ocy // nz + 2 * PAD) // 2)

    y_from = pl.multiple_of(cy - (cy - PAD) * sec, 8)
    y_to = pl.multiple_of((cy + PAD) * sec, 8)

    def y_copy(number, field):
        part = field.at[0:3, own]
        return copy_to(
            part.at[:, :, pl.ds(y_from, PAD)],
            part.at[:, :, pl.ds(y_to, PAD)],
            ys_sem.at[0], yr_sem.at[number], device(0, True),
        )

    x_s0 = chunks(S0, s0, s0_bounds, str_in)
    for part in x_s0:
        start(part)
    for copy in row_loads + loads + ocean_loads:
        copy.start()

    outer = pl.multiple_of((cy + PAD) * sec, 8)
    for field in (s0, s1):
        field[0:3, own, pl.ds(outer, PAD), :] = jnp.zeros((3, cx, PAD, nz), jnp.float32)
    for field in (v1, v2):
        field[:, own, pl.ds(outer, PAD), :] = jnp.zeros((3, cx, PAD, nz), jnp.float32)

    def clear(layers, orow, slot):
        for field in (s0, sp):
            field[XY : XX + 1, layers, rows_own, :] = jnp.zeros((3, LAY, cy, nz), jnp.float32)
        for field in (v1, v2):
            field[:, layers, rows_own, :] = jnp.zeros((3, LAY, cy, nz), jnp.float32)
        for field in (mu, stiff):
            field[layers] = jnp.zeros((LAY, cy, nz), jnp.float32)
        oce[:, orow, 0:ocy] = jnp.zeros((3, PAD, ocy), jnp.float32)
        dep[orow, 0:ocy] = jnp.zeros((PAD, ocy), jnp.float32)
        wet[orow, 0:ocy] = jnp.zeros((PAD, ocy), jnp.int32)
        locn[slot] = jnp.zeros(locn.shape[1:], jnp.float32)

    @pl.when(jnp.logical_not(has_low))
    def _():
        clear(slice(0, LAY), slice(0, PAD), 0)

    @pl.when(jnp.logical_not(has_high))
    def _():
        clear(slice(LAY + cx, LAY + cx + LAY), slice(PAD + ocx, PAD + ocx + PAD), 1)

    loc[...] = jnp.zeros(loc.shape, jnp.float32)
    for copy in row_loads:
        copy.wait()
    loc[0:1, 0:ocx] = src[...].astype(jnp.float32)
    loc[1:2, 0:ocx] = share[...]

    def ocean_rows(step, first, target, slot, index):
        return [
            copy_to(oce_in.at[:, pl.ds(first, PAD)], oce.at[:, pl.ds(target, PAD), 0:ocy], os_sem.at[index], or_sem.at[index], device(step)),
            copy_to(dep_in.at[pl.ds(first, PAD)], dep.at[pl.ds(target, PAD), 0:ocy], os_sem.at[index], or_sem.at[index], device(step)),
            copy_to(wet_in.at[pl.ds(first, PAD)], wet.at[pl.ds(target, PAD), 0:ocy], os_sem.at[index], or_sem.at[index], device(step)),
            copy_to(loc, locn.at[slot], os_sem.at[index], or_sem.at[index], device(step)),
        ]

    x_ocean = (
        ocean_rows(1, ocx - PAD, 0, 0, 0),
        ocean_rows(-1, 0, PAD + ocx, 1, 1),
    )
    wait_for(load_sem.at[0], 6, 2 * cx, cy)
    y_s0 = y_copy(0, s0)
    y_s0.start()

    buo[...] = TIME_STEP * buo[...]
    lam[...] = TIME_STEP * lam[...]
    mu[own] = TIME_STEP * mu[own]
    stiff[own] = lam[...] + 2.0 * mu[own]
    x_static = x_copies(STATIC, None)
    start(x_static)
    start(x_ocean)

    forward, backward = lane_coefs((1, 1, nz))

    def near_far(a, b, c, d):
        return NEAR_COEF * (a - b) + FAR_COEF * (c - d)

    def outer_x(a):
        zero = jnp.zeros_like(a[0:1])
        return jnp.concatenate([zero, zero, a, zero, zero])

    def forward_x(a):
        return near_far(a[3 : 3 + cx], a[2 : 2 + cx], a[4 : 4 + cx], a[1 : 1 + cx])

    def backward_x(a):
        return near_far(a[2 : 2 + cx], a[1 : 1 + cx], a[3 : 3 + cx], a[0:cx])

    every = pl.ds(0, cx + 2 * LAY)

    def place(g):
        begin = pl.multiple_of(8 * (g + sec * (groups - 1 - 2 * g)), 8)
        return pl.ds(begin, 8), begin + PAD

    def velocity_group(g, old, stress, new, halos, out=None):
        here, base = place(g)

        def at(c, layers=own, shift=0):
            return stress[c, layers, pl.ds(base + shift, 8), :]

        def fy(c):
            return near_far(at(c, own, 1), at(c), at(c, own, 2), at(c, own, -1))

        def by(c):
            return near_far(at(c), at(c, own, -1), at(c, own, 1), at(c, own, -2))

        def wide(c):
            return at(c, every) if halos else outer_x(at(c))

        scale = buo[:, here, :]
        x = forward_x(wide(XX)) + by(XY) + backward_z(at(XZ), backward)
        y = backward_x(wide(XY)) + fy(YY) + backward_z(at(YZ), backward)
        z = backward_x(wide(XZ)) + by(YZ) + forward_z(at(ZZ), forward)
        for c, value in enumerate((x, y, z)):
            if halos:
                result = old[c, own, pl.ds(base, 8), :] + scale * value
                new[c, own, pl.ds(base, 8), :] = result
                out[c, :, here, :] = result
            else:
                new[c, :, here, :] = old[c, :, here, :] + scale * value

    def stress_group(g, old, velocity, new, last):
        here, base = place(g)

        def at(c, shift=0):
            return velocity[c, own, pl.ds(base + shift, 8), :]

        def fy(c):
            return near_far(at(c, 1), at(c), at(c, 2), at(c, -1))

        strain_x = backward_x(outer_x(at(0)))
        strain_y = near_far(at(1), at(1, -1), at(1, 1), at(1, -2))
        strain_z = backward_z(at(2), backward)
        shear = mu[own, here, :]
        double = 2.0 * shear
        volume = lam[:, here, :] * (strain_x + strain_y + strain_z)
        change = {
            XX: volume + double * strain_x,
            YY: volume + double * strain_y,
            ZZ: volume + double * strain_z,
            XY: shear * (fy(0) + forward_x(outer_x(at(1)))),
            XZ: shear * (forward_z(at(0), forward) + forward_x(outer_x(at(2)))),
            YZ: shear * (forward_z(at(1), forward) + fy(2)),
        }
        for c, value in change.items():
            result = old[c, own, pl.ds(base, 8), :] + value
            if last:
                new[SOURCE[c], :, here, :] = result
            else:
                new[c, own, pl.ds(base, 8), :] = result

    forward_halo = {0: ((1, -FAR_COEF),), 2: ((6, FAR_COEF),), 3: ((6, NEAR_COEF), (7, FAR_COEF))}
    backward_halo = {0: ((1, -NEAR_COEF), (0, -FAR_COEF)), 1: ((1, -FAR_COEF),), 3: ((6, FAR_COEF),)}

    def weighted(field, c, terms, rows):
        total = None
        for layer, coef in terms:
            term = coef * field[c, layer, rows, :]
            total = term if total is None else total + term
        return total

    def velocity_halo(g, stress, partial, new):
        here, base = place(g)
        rows = pl.ds(base, 8)
        for c, (part, terms) in enumerate(((XX, forward_halo), (XY, backward_halo), (XZ, backward_halo))):
            for layer in range(cx):
                value = partial[c, layer, here, :]
                if layer in terms:
                    value = value + buo[layer, here, :] * weighted(stress, part, terms[layer], rows)
                new[c, low + layer, rows, :] = value

    def stress_halo(g, partial, velocity, new, last):
        here, base = place(g)
        rows = pl.ds(base, 8)

        def add(c, layer, value):
            if last:
                if value is not None:
                    new[SOURCE[c], layer, here, :] = new[SOURCE[c], layer, here, :] + value
            else:
                before = partial[c, low + layer, rows, :]
                new[c, low + layer, rows, :] = before if value is None else before + value

        for layer in range(cx):
            if layer in backward_halo:
                strain = weighted(velocity, 0, backward_halo[layer], rows)
                volume = lam[layer, here, :] * strain
                add(XX, layer, stiff[low + layer, here, :] * strain)
                add(YY, layer, volume)
                add(ZZ, layer, volume)
            else:
                for c in (XX, YY, ZZ):
                    add(c, layer, None)
            for c, part in ((XY, 1), (XZ, 2)):
                if layer in forward_halo:
                    add(c, layer, mu[low + layer, here, :] * weighted(velocity, part, forward_halo[layer], rows))
                else:
                    add(c, layer, None)
            add(YZ, layer, None)
        if last:
            return
        first, second, beneath, top = low, low + 1, high - 2, high - 1

        def complete(c, layer, coefs, part, terms):
            new[c, layer, rows, :] = partial[c, layer, rows, :] + coefs[layer, here, :] * weighted(velocity, part, terms, rows)

        complete(XX, 1, stiff, 0, ((first, FAR_COEF),))
        complete(XX, high, stiff, 0, ((top, -NEAR_COEF), (beneath, -FAR_COEF)))
        complete(XX, high + 1, stiff, 0, ((top, -FAR_COEF),))
        for c, part in ((XY, 1), (XZ, 2)):
            complete(c, 0, mu, part, ((first, FAR_COEF),))
            complete(c, 1, mu, part, ((first, NEAR_COEF), (second, FAR_COEF)))
            complete(c, high, mu, part, ((top, -FAR_COEF),))

    def each(first, last, function, *args):
        def body(g, carry):
            function(g, *args)
            return carry

        lax.fori_loop(first, last, body, 0)

    def each_edge_first(first, last, copy, function, *args):
        def body(p, carry):
            function(jnp.where(p == first, last - 1, p - 1), *args)

            @pl.when(p == first)
            def _():
                copy.start()

            return carry

        lax.fori_loop(first, last, body, 0)

    def each_edge_last(first, last, copy, function, *args):
        def body(g, carry):
            @pl.when(g == last - 1)
            def _():
                copy.wait_recv()

            function(g, *args)
            return carry

        lax.fori_loop(first, last, body, 0)

    each_edge_last(0, groups, y_s0, velocity_group, v0, s0, v0, False)
    x_v1, y_v1 = chunks(V1, v1, s0_bounds), y_copy(1, v1)
    x_sp, y_s1 = chunks(SP, sp, sp_bounds), y_copy(2, s1)
    parts = len(s0_bounds) - 1
    for i in range(parts):
        final = i == parts - 1
        arrive(x_s0[i])
        if final:
            each_edge_first(s0_bounds[i], groups, y_v1, velocity_halo, s0, v0, v1)
        else:
            each(s0_bounds[i], s0_bounds[i + 1], velocity_halo, s0, v0, v1)
        start(x_v1[i])
        if final:
            each_edge_last(sp_bounds[i], groups, y_v1, stress_group, s0, v1, sp, False)
        elif sp_bounds[i] < sp_bounds[i + 1]:
            each(sp_bounds[i], sp_bounds[i + 1], stress_group, s0, v1, sp, False)
        start(x_sp[i])

    wait_for(load_sem.at[1], 5, ocx * ocy // (nz * cy), cy)
    pl.when(has_low)(lambda: ocean_wait(or_sem.at[0]))
    pl.when(has_high)(lambda: ocean_wait(or_sem.at[1]))
    edge = pl.multiple_of(half * (1 - sec), 128)

    def ocean_columns(field):
        where = (slice(None),) * (len(field.shape) - 1)
        a, b = field.at[(*where, pl.ds(edge, half))], field.at[(*where, pl.ds(ocy, half))]
        return copy_to(a, b, os_sem.at[2], or_sem.at[2], device(0, True))

    y_ocean = [ocean_columns(oce), ocean_columns(dep), ocean_columns(wet)]
    for copy in y_ocean:
        copy.start()

    lane = lax.broadcasted_iota(jnp.int32, (8, 128), 1)

    def spread(value):
        return jnp.broadcast_to(value, (8, 128))

    def lanes_of(index):
        mine = pltpu.roll(spread(loc[index : index + 1, :]), PAD, 1)
        below = pltpu.roll(spread(locn[0, index : index + 1, :]), 128 - (ocx - PAD), 1)
        above = pltpu.roll(spread(locn[1, index : index + 1, :]), PAD + ocx, 1)
        return jnp.where(lane < PAD, below, jnp.where(lane < PAD + ocx, mine, above))

    slot = lax.broadcasted_iota(jnp.int32, (8, 128), 0)
    picked = lanes_of(0).astype(jnp.int32) - tile + FAR_REACH == slot
    row[...] = jnp.where(picked, OCEAN_STEP * lanes_of(1), 0.0)

    for sem in (or_sem.at[2], os_sem.at[2]):
        wait_for(sem, 1, 5, ocx + 2 * PAD)
    region = oce.shape[1:]
    width = region[1]
    lanes = lax.broadcasted_iota(jnp.int32, (1, width), 1)
    beyond = lanes - ocy
    inside = (beyond < 0) | ((beyond < half // 2) & (sec == 0)) | ((beyond >= half // 2) & (sec == 1))
    rows = lax.broadcasted_iota(jnp.int32, (region[0], 1), 0)
    inside_rows = ((rows >= PAD) | has_low) & ((rows < PAD + ocx) | has_high)
    mask = inside.astype(jnp.float32) * inside_rows.astype(jnp.float32)
    wetf = wet[...].astype(jnp.float32) * mask
    vel1[3] = wetf
    oce[0] = oce[0] * mask
    HALF_STEP = 0.5 * OCEAN_STEP

    def ocean_flow(eta, u, v, first, count, out_u, out_v):
        here = pl.ds(first, count)
        middle = eta[here, :]
        w = vel1[3, here, :]
        new_u = w * (u[here, :] - HALF_STEP * (eta[pl.ds(first + 1, count), :] - eta[pl.ds(first - 1, count), :]))
        new_v = w * (v[here, :] - HALF_STEP * (pltpu.roll(middle, width - 1, 1) - pltpu.roll(middle, 1, 1)))
        out_u[here, :] = new_u
        out_v[here, :] = new_v
        flux[0, here, :] = dep[here, :] * new_u
        flux[1, here, :] = dep[here, :] * new_v

    def ocean_fall(first, count):
        along = flux[1, pl.ds(first, count), :]
        return HALF_STEP * (
            flux[0, pl.ds(first + 1, count), :] - flux[0, pl.ds(first - 1, count), :]
            + pltpu.roll(along, width - 1, 1) - pltpu.roll(along, 1, 1)
        )

    ocean_flow(oce.at[0], oce.at[1], oce.at[2], 4, ocx + 8, vel1.at[0], vel1.at[1])
    here = pl.ds(5, ocx + 6)
    rows_here = lax.broadcasted_iota(jnp.int32, (ocx + 6, 1), 0) + 5
    mask_here = inside.astype(jnp.float32) * (
        ((rows_here >= PAD) | has_low) & ((rows_here < PAD + ocx) | has_high)
    ).astype(jnp.float32)
    vel1[2, here, :] = (oce[0, here, :] - ocean_fall(5, ocx + 6)) * mask_here

    arrive(x_static)
    x_v2, y_v2 = chunks(V2, v2, v2_bounds), y_copy(3, v2)
    for i in range(parts):
        final = i == parts - 1
        arrive(x_v1[i])
        arrive(x_sp[i])
        if final:
            each_edge_first(sp_bounds[i], groups, y_s1, stress_halo, sp, v1, s1, False)
            each_edge_last(v2_bounds[i], groups, y_s1, velocity_group, v1, s1, v2, True, vel_out)
        else:
            if sp_bounds[i] < sp_bounds[i + 1]:
                each(sp_bounds[i], sp_bounds[i + 1], stress_halo, sp, v1, s1, False)
            if v2_bounds[i] < v2_bounds[i + 1]:
                each(v2_bounds[i], v2_bounds[i + 1], velocity_group, v1, s1, v2, True, vel_out)
        start(x_v2[i])
    y_v2.start()

    top = v2[2, own, rows_own, :].reshape(cx * cy, nz)
    first_lane = (lax.broadcasted_iota(jnp.int32, (8, nz), 1) == 0).astype(jnp.float32)
    patch = lax.dot_general(
        first_lane, top, (((1,), (1,)), ((), ())),
        precision=lax.Precision.HIGHEST, preferred_element_type=jnp.float32,
    )
    pat[8:16, 0:ocy] = patch
    patch_copies = []
    for other in (False, True):
        for step in range(-FAR_REACH, FAR_REACH + 1):
            if step == 0 and not other:
                continue
            index = FAR_REACH - step
            if other:
                source = pat.at[8:9, pl.ds(edge, half)]
                target = pat.at[index : index + 1, ocy : ocy + half]
            else:
                source = pat.at[8:9, 0:ocy]
                target = pat.at[index : index + 1, 0:ocy]
            copy = copy_to(source, target, ps_sem.at[int(other), index], pr_sem.at[int(other), index], device(step, other))
            back = (tile - step >= 0) & (tile - step < tiles)
            ahead = (tile + step >= 0) & (tile + step < tiles)
            patch_copies.append((copy, ahead, back))
    for copy, ahead, back in patch_copies:
        pl.when(ahead)(copy.start)
    pat[FAR_REACH : FAR_REACH + 1, 0:ocy] = patch[0:1]

    each_edge_last(0, groups, y_v2, stress_group, s1, v2, str_out, True)
    for i in range(parts):
        arrive(x_v2[i])
    each(0, groups, stress_halo, None, v2, str_out, True)

    for copy, ahead, back in patch_copies:
        pl.when(back)(copy.wait_recv)
    uplift = lax.dot_general(
        row[...], pat[0:8, :], (((0,), (0,)), ((), ())),
        precision=lax.Precision.HIGHEST, preferred_element_type=jnp.float32,
    )[0 : PAD + ocx + PAD]
    source = vel1[3] * uplift
    oce[0] = vel1[2] + source
    ocean_flow(oce.at[0], vel1.at[0], vel1.at[1], PAD - 1, ocx + 2, oce.at[1], oce.at[2])
    oce_out[0] = oce[0, orow_own, 0:ocy] - ocean_fall(PAD, ocx)[:, 0:ocy] + source[PAD : PAD + ocx, 0:ocy]
    oce_out[1:3] = oce[1:3, orow_own, 0:ocy]

    @pl.when(has_high)
    def _():
        wait_for(xs_sem.at[0], 3, 7, cy)
        ocean_wait(os_sem.at[0])

    @pl.when(has_low)
    def _():
        wait_for(xs_sem.at[1], 3, 7, cy)
        ocean_wait(os_sem.at[1])

    wait_for(ys_sem.at[0], 6, 8, 2 * cx)
    for copy, ahead, back in patch_copies:
        pl.when(ahead)(copy.wait_send)


def store(velocity, stresses, ocean, vel_out, str_out, oce_out, sem):
    copies = [
        pltpu.make_async_copy(a, b, sem.at[i])
        for i, (a, b) in enumerate(((stresses, str_out), (velocity, vel_out), (ocean, oce_out)))
    ]
    for copy in copies:
        copy.start()
    for copy in copies:
        copy.wait()


def solution(mesh):
    tiles = mesh.shape["tile"]

    def shards(velocity, stresses, buoyancy, lame_first, shear_mod, ocean_state, depth_map, wet_mask, src, share):
        cx, cy, nz = buoyancy.shape
        ocx, ocy = depth_map.shape
        layers, rows = cx + 2 * LAY, cy + 2 * PAD
        region = (ocx + 2 * PAD, ocy + ocy // 2)
        hbm = pl.BlockSpec(memory_space=pltpu.HBM)
        vmem = pl.BlockSpec(memory_space=pltpu.VMEM)
        dma = pltpu.SemaphoreType.DMA
        f32 = jnp.float32
        results = pl.pallas_call(
            functools.partial(kernel, tiles),
            out_shape=(
                jax.ShapeDtypeStruct(velocity.shape, f32),
                jax.ShapeDtypeStruct(stresses.shape, f32),
                jax.ShapeDtypeStruct(ocean_state.shape, f32),
            ),
            in_specs=[hbm] * 10,
            out_specs=(vmem,) * 3,
            scratch_shapes=[
                pltpu.VMEM((6, layers, rows, nz), f32),
                pltpu.VMEM((6, layers, rows, nz), f32),
                pltpu.VMEM((6, layers, rows, nz), f32),
                pltpu.VMEM(velocity.shape, f32),
                pltpu.VMEM((3, layers, rows, nz), f32),
                pltpu.VMEM((3, layers, rows, nz), f32),
                pltpu.VMEM(buoyancy.shape, f32),
                pltpu.VMEM(buoyancy.shape, f32),
                pltpu.VMEM((layers, cy, nz), f32),
                pltpu.VMEM((layers, cy, nz), f32),
                pltpu.VMEM((1, ocx), jnp.int32),
                pltpu.VMEM((1, ocx), f32),
                pltpu.VMEM((3, *region), f32),
                pltpu.VMEM(region, f32),
                pltpu.VMEM(region, jnp.int32),
                pltpu.VMEM((2 * PAD, 128), f32),
                pltpu.VMEM((2, 2 * PAD, 128), f32),
                pltpu.VMEM((16, region[1]), f32),
                pltpu.VMEM((8, 128), f32),
                pltpu.VMEM((2, *region), f32),
                pltpu.VMEM((4, *region), f32),
                dma((2,)),
                dma((2,)),
                dma((2,)),
                dma((5, len(BOUNDS) - 1, 2)),
                dma((1,)),
                dma((4,)),
                dma((3,)),
                dma((3,)),
                dma((2, 7)),
                dma((2, 7)),
            ],
            compiler_params=pltpu.CompilerParams(
                collective_id=0, has_side_effects=True, vmem_limit_bytes=40 * 1024 * 1024
            ),
        )(
            *(
                pltpu.with_memory_space_constraint(array, pltpu.HBM)
                for array in (
                    velocity, stresses, buoyancy, lame_first, shear_mod, ocean_state, depth_map, wet_mask,
                    src.reshape(1, ocx), share.reshape(1, ocx),
                )
            )
        )
        return pl.pallas_call(
            store,
            out_shape=tuple(jax.ShapeDtypeStruct(r.shape, f32) for r in results),
            in_specs=[vmem] * 3,
            out_specs=(hbm,) * 3,
            scratch_shapes=[dma((3,))],
            compiler_params=pltpu.CompilerParams(vmem_limit_bytes=8 * 1024 * 1024),
        )(*results)

    return jax.shard_map(
        shards,
        mesh=mesh,
        in_specs=(
            P(None, "tile", "sec", None),
            P(None, "tile", "sec", None),
            P("tile", "sec", None),
            P("tile", "sec", None),
            P("tile", "sec", None),
            P(None, "tile", "sec"),
            P("tile", "sec"),
            P("tile", "sec"),
            P("tile"),
            P("tile"),
        ),
        out_specs=(
            P(None, "tile", "sec", None),
            P(None, "tile", "sec", None),
            P(None, "tile", "sec"),
        ),
        check_vma=False,
    )
```
